32 devices in a mesh: frames: 8 (over y, x, core), heads: 4 (over z).
Axes of the slice: x: 2, y: 2, z: 4, core: 2. Of those that a mesh axis runs over, the one named last changes fastest.
Arguments:
- frames_in: bfloat16 [64, 197, 768], P('frames', None, 'heads'), may hold values from -6 to 6
- upstream: bfloat16 [64, 197, 768], P('frames', None, 'heads'), may hold values from -6 to 6
- video_of_frame: int32 [64], replicated, may hold values from 0 to 11, never falling along the last dimension, each value on 1 to 8 neighbouring positions
- group_ids: int32 [12], replicated, may hold values from 0 to 3
- msg_fc_weight: bfloat16 [768, 768], P('heads'), may hold values from -0.21875 to 0.21875
- msg_fc_bias: bfloat16 [768], P('heads'), may hold values from -1.75 to 1.75
- msg_gain: bfloat16 [768], P('heads'), may hold values from 0.5 to 1.5
- msg_shift: bfloat16 [768], P('heads'), may hold values from -1.75 to 1.75
- msg_qkv_weight: bfloat16 [768, 3, 768], P(None, None, 'heads'), may hold values from -0.21875 to 0.21875
- msg_qv_bias: bfloat16 [2, 768], P(None, 'heads'), may hold values from -1.75 to 1.75
- courier_result_kernel: bfloat16 [768, 768], P('heads'), may hold values from -0.4375 to 0.4375
- msg_out_bias: bfloat16 [768], P('heads'), may hold values from -1.75 to 1.75
- ln1_gain: bfloat16 [768], P('heads'), may hold values from 0.5 to 1.5
- ln1_shift: bfloat16 [768], P('heads'), may hold values from -1.75 to 1.75
- qkv_weight: bfloat16 [768, 3, 768], P(None, None, 'heads'), may hold values from -0.21875 to 0.21875
- qv_bias: bfloat16 [2, 768], P(None, 'heads'), may hold values from -1.75 to 1.75
- picture_result_kernel: bfloat16 [768, 768], P('heads'), may hold values from -0.875 to 0.875
- out_bias: bfloat16 [768], P('heads'), may hold values from -1.75 to 1.75
- ln2_gain: bfloat16 [768], P('heads'), may hold values from 0.5 to 1.5
- ln2_shift: bfloat16 [768], P('heads'), may hold values from -1.75 to 1.75
- fc_weight: bfloat16 [768, 3072], P(None, 'heads'), may hold values from -0.21875 to 0.21875
- fc_bias: bfloat16 [3072], P('heads'), may hold values from -1.75 to 1.75
- proj_weight: bfloat16 [3072, 768], P('heads'), may hold values from -0.15625 to 0.15625
- proj_bias: bfloat16 [768], P('heads'), may hold values from -1.75 to 1.75
Outputs:
- output: bfloat16 [64, 197, 768], P('frames', None, 'heads')
- loss: float32 [], replicated
- grad_input: float32 [64, 197, 768], P('frames', None, 'heads')
- grad_msg_fc_weight: float32 [768, 768], P('heads')
- grad_msg_fc_bias: float32 [768], P('heads')
- grad_msg_gain: float32 [768], P('heads')
- grad_msg_shift: float32 [768], P('heads')
- grad_msg_qkv_weight: float32 [768, 3, 768], P(None, None, 'heads')
- grad_msg_qv_bias: float32 [2, 768], P(None, 'heads')
- grad_msg_out_weight: float32 [768, 768], P('heads')
- grad_msg_out_bias: float32 [768], P('heads')
- first_norm_gain_gradient: float32 [768], P('heads')
- grad_ln1_shift: float32 [768], P('heads')
- grad_qkv_weight: float32 [768, 3, 768], P(None, None, 'heads')
- grad_qv_bias: float32 [2, 768], P(None, 'heads')
- grad_out_weight: float32 [768, 768], P('heads')
- grad_out_bias: float32 [768], P('heads')
- grad_ln2_gain: float32 [768], P('heads')
- grad_ln2_shift: float32 [768], P('heads')
- grad_fc_weight: float32 [768, 3072], P(None, 'heads')
- grad_fc_bias: float32 [3072], P('heads')
- grad_proj_weight: float32 [3072, 768], P('heads')
- grad_proj_bias: float32 [768], P('heads')
The draws below stay inside these ranges and needn't reach their ends.
Inputs may be any that keep to these rules, and one draw needn't show every extreme that they name: `video_of_frame`: video ids never fall along the frames; every video has 1 to 8 frames, and some video has exactly 8.
All inputs are finite; a program needn't handle non-finite values.
Results may differ from the reference program's by a relative error of at most 0.025.
Values may be sent and summed in bfloat16 or wider, within the bound.
No kernel may reach another device: no remote copies, remote signals or barrier semaphores. Data moves between devices by JAX's collectives and lax.ppermute only.
A program may use at most 128 MiB of HBM per device.

```python
import math
import jax
import jax.numpy as jnp
import numpy as np
from jax import lax

D = 768
HEADS = 12
HS = 64
FF = 3072
PATCHES = 197
MAXF = 8
FRAMES = 64
VIDEOS = 12
GROUPS = 4


def place_ends(drawn, rng, low, largest):
    place = [jax.random.randint(jax.random.fold_in(rng, axis), (), 0, length) for axis, length in enumerate(drawn.shape)]
    widest = drawn.shape.index(max(drawn.shape))
    beside = place[:widest] + [(place[widest] + 1) % drawn.shape[widest]] + place[widest + 1:]
    return drawn.at[tuple(place)].set(low).at[tuple(beside)].set(largest)


def level_of(key, shape, shards, low, largest):
    def one(dim, blocks):
        heights = jax.random.uniform(jax.random.fold_in(jax.random.fold_in(key, 6), dim), (blocks,), jnp.float32, low / len(shards), largest / len(shards))
        return jnp.repeat(jnp.exp(heights), shape[dim] // blocks).reshape((-1,) + (1,) * (len(shape) - dim - 1))

    loudness = one(*shards[0])
    for cut in shards[1:]:
        loudness = loudness * one(*cut)
    return loudness


def profile(count, total, limit, skew):
    loads = [(1 << 20) // math.isqrt(standing ** skew) + 1 for standing in range(2, count + 1)]
    spare, counts = total - limit - (count - 1), [1] * (count - 1)
    while spare > 0:
        free = [i for i in range(count - 1) if counts[i] < limit]
        pool, remaining = sum([loads[i] for i in free]), spare
        for i in free:
            more = min(limit - counts[i], max(1, remaining * loads[i] // pool), spare)
            counts[i] = counts[i] + more
            spare = spare - more
    return np.array([limit] + counts)


def ragged_sizes(stream_key, amount, total, most, skew):
    if amount == 2:
        one = jax.random.randint(stream_key, (), max(1, total - most), min(most, total - 1) + 1)
        return jnp.stack([one, total - one])
    lengths = jnp.asarray(profile(amount, total, most, skew), jnp.int32)
    pairs = (amount - 1) // 2
    donor, receiver = lengths[1:1 + 2 * pairs:2], lengths[2:2 + 2 * pairs:2]
    slack = jnp.minimum(donor - 1, most - receiver)
    moved = jax.random.randint(jax.random.fold_in(stream_key, 1), (pairs,), 0, 1 << 20) % (slack + 1)
    lengths = lengths.at[1:1 + 2 * pairs:2].set(donor - moved).at[2:2 + 2 * pairs:2].set(receiver + moved)
    return lengths[jax.random.permutation(jax.random.fold_in(stream_key, 2), amount)]


def normal_values(stream_key, shape, scale, reach, split=(), kind=jnp.bfloat16):
    result = scale * jax.random.normal(stream_key, shape, jnp.float32)
    if split:
        result = result * level_of(stream_key, shape, split, -0.22, 0.18)
    return jnp.clip(result, -reach, reach).astype(kind)


def setup_inputs(seed: int = 0) -> dict:
    splits = jax.random.split(jax.random.key(seed), 25)
    frames_in = normal_values(splits[0], (FRAMES, PATCHES, D), 1.0, 6.0, ((0, 8), (2, 4)))
    upstream = normal_values(splits[1], (FRAMES, PATCHES, D), 1.0, 6.0, ((0, 8), (2, 4)))
    video_of_frame = jnp.searchsorted(jnp.cumsum(ragged_sizes(splits[2], VIDEOS, FRAMES, MAXF, 1)), jnp.arange(FRAMES), side="right").astype(jnp.int32)
    group_ids = place_ends(jax.random.randint(splits[3], (VIDEOS,), 0, GROUPS), jax.random.fold_in(splits[3], 1), 0, GROUPS - 1).astype(jnp.int32)
    msg_fc_weight = normal_values(splits[4], (D, D), D ** -0.5, 0.21875, ((0, 4),))
    msg_fc_bias = normal_values(splits[5], (D,), 0.3, 1.75, ((0, 4),))
    msg_gain = jnp.clip(1.0 + 0.1 * jax.random.normal(splits[6], (D,), jnp.float32), 0.5, 1.5).astype(jnp.bfloat16)
    msg_shift = normal_values(splits[7], (D,), 0.3, 1.75, ((0, 4),))
    msg_qkv_weight = normal_values(splits[8], (D, 3, D), D ** -0.5, 0.21875, ((2, 4),))
    msg_qv_bias = normal_values(splits[9], (2, D), 0.3, 1.75, ((1, 4),))
    courier_result_kernel = normal_values(splits[10], (D, D), (D // 4) ** -0.5, 0.4375, ((0, 4),))
    msg_out_bias = normal_values(splits[11], (D,), 0.3, 1.75, ((0, 4),))
    ln1_gain = jnp.clip(1.0 + 0.1 * jax.random.normal(splits[12], (D,), jnp.float32), 0.5, 1.5).astype(jnp.bfloat16)
    ln1_shift = normal_values(splits[13], (D,), 0.3, 1.75, ((0, 4),))
    qkv_weight = normal_values(splits[14], (D, 3, D), D ** -0.5, 0.21875, ((2, 4),))
    qv_bias = normal_values(splits[15], (2, D), 0.3, 1.75, ((1, 4),))
    picture_result_kernel = normal_values(splits[16], (D, D), (D // 14) ** -0.5, 0.875, ((0, 4),))
    out_bias = normal_values(splits[17], (D,), 0.3, 1.75, ((0, 4),))
    ln2_gain = jnp.clip(1.0 + 0.1 * jax.random.normal(splits[18], (D,), jnp.float32), 0.5, 1.5).astype(jnp.bfloat16)
    ln2_shift = normal_values(splits[19], (D,), 0.3, 1.75, ((0, 4),))
    fc_weight = normal_values(splits[20], (D, FF), D ** -0.5, 0.21875, ((1, 4),))
    fc_bias = normal_values(splits[21], (FF,), 0.3, 1.75, ((0, 4),))
    proj_weight = normal_values(splits[22], (FF, D), (FF // 2) ** -0.5, 0.15625, ((0, 4),))
    proj_bias = normal_values(splits[23], (D,), 0.3, 1.75, ((0, 4),))
    return dict(frames_in=frames_in, upstream=upstream, video_of_frame=video_of_frame, group_ids=group_ids, msg_fc_weight=msg_fc_weight, msg_fc_bias=msg_fc_bias, msg_gain=msg_gain, msg_shift=msg_shift, msg_qkv_weight=msg_qkv_weight, msg_qv_bias=msg_qv_bias, courier_result_kernel=courier_result_kernel, msg_out_bias=msg_out_bias, ln1_gain=ln1_gain, ln1_shift=ln1_shift, qkv_weight=qkv_weight, qv_bias=qv_bias, picture_result_kernel=picture_result_kernel, out_bias=out_bias, ln2_gain=ln2_gain, ln2_shift=ln2_shift, fc_weight=fc_weight, fc_bias=fc_bias, proj_weight=proj_weight, proj_bias=proj_bias)


@jax.custom_vjp
def low(v):
    return lax.optimization_barrier(v.astype(jnp.bfloat16)).astype(jnp.float32)

@jax.custom_vjp
def low_back(v):
    return v

def low_keep(v):
    return (low(v), None)

def low_pass(kept, grad):
    return (grad,)

def back_keep(v):
    return (v, None)

def back_low(kept, grad):
    return (low(grad),)
low.defvjp(low_keep, low_pass)
low_back.defvjp(back_keep, back_low)
norm_eps = 1e-05
score_scale = 0.125
gelu_rate = 1.702
contrast_sharpness = 0.02
masked_score = -1000000000.0
largest_cosine_score = lax.Precision.HIGHEST

def product(left, right):
    return jnp.matmul(left, right, precision=largest_cosine_score)

def layer_norm(values, gain, shift):
    center = lax.optimization_barrier(jnp.mean(values, axis=-1, keepdims=True))
    offset = values - center
    spread = lax.optimization_barrier(jnp.mean(offset * offset, axis=-1, keepdims=True))
    return offset * lax.rsqrt(spread + norm_eps) * gain + shift

def contrast_loss(pooled_sum, frame_counts, group_ids):
    video_count = group_ids.shape[0]
    pooled = pooled_sum / frame_counts[:, None]
    direction_embeddings = pooled * lax.rsqrt(lax.optimization_barrier(jnp.sum(pooled * pooled, axis=1, keepdims=True)) + 1e-06)
    cosine_score_table = jnp.matmul(direction_embeddings, direction_embeddings.T, precision=largest_cosine_score) / contrast_sharpness
    video_list = jnp.arange(video_count, dtype=jnp.int32)
    itself = video_list[:, None] == video_list[None, :]
    cosine_score_table = jnp.where(itself, masked_score, cosine_score_table)
    log_total = jax.nn.logsumexp(cosine_score_table, axis=1)
    positive = jnp.logical_and(group_ids[:, None] == group_ids[None, :], jnp.logical_not(itself)).astype(jnp.float32)
    pos_count = jnp.maximum(lax.optimization_barrier(jnp.sum(positive, axis=1)), 1.0)
    per_anchor = lax.optimization_barrier(jnp.sum(positive * (log_total[:, None] - cosine_score_table), axis=1)) / pos_count
    return jnp.sum(per_anchor)

def message_part(inputs, video_of_frame, params):
    fc_weight, fc_bias, gain, shift, qkv_weight, qv_bias, picture_result_kernel, out_bias = params
    frame_total = inputs.shape[0]
    start = low_back(product(inputs[:, 0, :], fc_weight) + fc_bias)
    normed = low(layer_norm(start, gain, shift))
    queries = low(low_back(product(normed, qkv_weight[:, 0, :]) + qv_bias[0])).reshape(frame_total, HEADS, HS)
    keys_in = low(low_back(product(normed, qkv_weight[:, 1, :]))).reshape(frame_total, HEADS, HS)
    values_in = low(low_back(product(normed, qkv_weight[:, 2, :]) + qv_bias[1])).reshape(frame_total, HEADS, HS)
    same_video = video_of_frame[:, None] == video_of_frame[None, :]
    scores = low_back(jnp.einsum('qhd,khd->hqk', queries, keys_in, precision=largest_cosine_score) * score_scale)
    scores = jnp.where(same_video[None], scores, masked_score)
    probs = low(jax.nn.softmax(scores, axis=-1))
    context = jnp.einsum('hqk,khd->qhd', probs, values_in, precision=largest_cosine_score)
    context = low(low_back(context)).reshape(frame_total, D)
    attended = low_back(product(context, picture_result_kernel) + out_bias)
    return start + attended

def frame_part(stream_one, params):
    gain_one, shift_one, qkv_weight, qv_bias, picture_result_kernel, out_bias, gain_two, shift_two, fc_weight, fc_bias, proj_weight, proj_bias = params
    block, tokens, width = stream_one.shape
    normed = low(layer_norm(stream_one, gain_one, shift_one))
    queries = low(low_back(product(normed, qkv_weight[:, 0, :]) + qv_bias[0])).reshape(block, tokens, HEADS, HS)
    keys_in = low(low_back(product(normed, qkv_weight[:, 1, :]))).reshape(block, tokens, HEADS, HS)
    values_in = low(low_back(product(normed, qkv_weight[:, 2, :]) + qv_bias[1])).reshape(block, tokens, HEADS, HS)
    scores = low_back(jnp.einsum('fqhd,fkhd->fhqk', queries, keys_in, precision=largest_cosine_score) * score_scale)
    probs = low(jax.nn.softmax(scores, axis=-1))
    context = jnp.einsum('fhqk,fkhd->fqhd', probs, values_in, precision=largest_cosine_score)
    context = low(low_back(context)).reshape(block, tokens, width)
    attended = low_back(product(context, picture_result_kernel) + out_bias)
    stream_two = stream_one[:, :PATCHES] + attended[:, :PATCHES]
    mlp_in = low(layer_norm(stream_two, gain_two, shift_two))
    hidden_pre = low_back(product(mlp_in, fc_weight) + fc_bias)
    hidden = low(hidden_pre * jax.nn.sigmoid(gelu_rate * hidden_pre))
    mlp_out = low_back(product(hidden, proj_weight) + proj_bias)
    return stream_two + mlp_out

def forward(inputs, params, video_of_frame, group_ids):
    final_message = message_part(inputs, video_of_frame, params[:8])
    stream_one = jnp.concatenate([inputs, final_message[:, None, :]], axis=1)
    frame_total = inputs.shape[0]
    blocks = stream_one.reshape(frame_total // 16, 16, PATCHES + 1, D)

    def run_block(block_in):
        return frame_part(block_in, params[8:])
    stream_three = lax.map(jax.checkpoint(run_block), blocks).reshape(frame_total, PATCHES, D)
    video_list = jnp.arange(VIDEOS, dtype=jnp.int32)
    onehot = (video_of_frame[None, :] == video_list[:, None]).astype(jnp.float32)
    frame_counts = lax.optimization_barrier(jnp.sum(onehot, axis=1))
    pooled_sum = product(onehot, stream_three[:, 0, :])
    return (stream_three, contrast_loss(pooled_sum, frame_counts, group_ids))

def reference(frames_in, upstream, video_of_frame, group_ids, msg_fc_weight, msg_fc_bias, msg_gain, msg_shift, msg_qkv_weight, msg_qv_bias, courier_result_kernel, msg_out_bias, ln1_gain, ln1_shift, qkv_weight, qv_bias, picture_result_kernel, out_bias, ln2_gain, ln2_shift, fc_weight, fc_bias, proj_weight, proj_bias):
    params = tuple((weight.astype(jnp.float32) for weight in (msg_fc_weight, msg_fc_bias, msg_gain, msg_shift, msg_qkv_weight, msg_qv_bias, courier_result_kernel, msg_out_bias, ln1_gain, ln1_shift, qkv_weight, qv_bias, picture_result_kernel, out_bias, ln2_gain, ln2_shift, fc_weight, fc_bias, proj_weight, proj_bias)))
    inputs = frames_in.astype(jnp.float32)

    def objective(inputs_now, params_now):
        return forward(inputs_now, params_now, video_of_frame, group_ids)
    results, pullback = jax.vjp(objective, inputs, params)
    stream_three, loss_value = results
    grad_input, grads = pullback((upstream.astype(jnp.float32), jnp.ones((), jnp.float32)))
    g_msg_fc_w, g_msg_fc_b, g_msg_gain, g_msg_shift, g_msg_qkv, g_msg_qvb, g_msg_out_w, g_msg_out_b, g_ln1_gain, g_ln1_shift, g_qkv, g_qvb, g_out_w, g_out_b, g_ln2_gain, g_ln2_shift, g_fc_w, g_fc_b, g_proj_w, g_proj_b = grads
    return (stream_three.astype(jnp.bfloat16), loss_value, grad_input, g_msg_fc_w, g_msg_fc_b, g_msg_gain, g_msg_shift, g_msg_qkv, g_msg_qvb, g_msg_out_w, g_msg_out_b, g_ln1_gain, g_ln1_shift, g_qkv, g_qvb, g_out_w, g_out_b, g_ln2_gain, g_ln2_shift, g_fc_w, g_fc_b, g_proj_w, g_proj_b)
```

```python
import functools

import jax
import jax.numpy as jnp
from jax import lax
from jax.experimental import pallas as pl
from jax.experimental.pallas import tpu as pltpu
from jax.sharding import PartitionSpec as P

HS = 64
GROUP = 8

norm_eps = 1e-05
score_scale = 0.125
gelu_rate = 1.702
contrast_sharpness = 0.02
masked_score = -1000000000.0
exact = lax.Precision.HIGHEST
f32 = jnp.float32
bf16 = jnp.bfloat16

PIECES = ((0, 2, 4, 6), (0, 4, 2, 6))


def nn(left, right):
    return lax.dot_general(left, right, (((1,), (0,)), ((), ())), preferred_element_type=f32)


def nt(left, right):
    return lax.dot_general(left, right, (((1,), (1,)), ((), ())), preferred_element_type=f32)


def tn(left, right):
    return lax.dot_general(left, right, (((0,), (0,)), ((), ())), preferred_element_type=f32)


def to_heads(value, step):
    count = lax.axis_size("heads")
    return lax.ppermute(value, "heads", [(i, (i + step) % count) for i in range(count)])


def swap_frames(value, bit):
    count = lax.axis_size("frames")
    return lax.ppermute(value, "frames", [(i, i ^ bit) for i in range(count)])


def frame_bits(start=1):
    count = lax.axis_size("frames")
    bits = []
    bit = start
    while bit < count:
        bits.append(bit)
        bit *= 2
    return bits


def in_order(slots, head_index):
    count = len(slots)
    return [
        lax.select_n(jnp.mod(head_index - block, count).astype(jnp.int32), *slots)
        for block in range(count)
    ]


def all_frames(value):
    for bit in frame_bits():
        value = jnp.concatenate([value, swap_frames(value, bit)], axis=0)
    return value


def norm_stats(rows):
    center = jnp.mean(rows, axis=-1, keepdims=True)
    offset = rows - center
    factor = lax.rsqrt(jnp.mean(offset * offset, axis=-1, keepdims=True) + norm_eps)
    return offset * factor, factor


def norm_back(grad_out, normed, factor, gain):
    scaled = grad_out * gain
    first = jnp.mean(scaled, axis=-1, keepdims=True)
    second = jnp.mean(scaled * normed, axis=-1, keepdims=True)
    grad_in = factor * (scaled - first - normed * second)
    return (
        grad_in,
        jnp.sum(grad_out * normed, axis=0, keepdims=True),
        jnp.sum(grad_out, axis=0, keepdims=True),
    )


def place_weight(target, own, near, far, place, slot):
    block = target.shape[0] // GROUP
    half = block // 2

    @pl.when(slot == 0)
    def _():
        target[...] = own[...]

    @pl.when(slot > 0)
    def _():
        for q in range(2):
            for j in range(4):
                here = (place ^ PIECES[q][j]) * block + q * half
                there = (place ^ PIECES[q][j] ^ 1) * block + q * half
                target[pl.ds(pl.multiple_of(here, 16), half), :] = near[q, j]
                target[pl.ds(pl.multiple_of(there, 16), half), :] = far[q, j]


def spread_grad(keep, send, value, place):
    block = value.shape[0] // GROUP
    for owner in range(GROUP):
        part = value[owner * block : (owner + 1) * block].astype(bf16)
        offset = place ^ owner
        rest = offset // 2
        mine = offset % 2 == 0

        @pl.when(mine)
        def _():
            keep[rest % 2, rest // 2] = part

        @pl.when(jnp.logical_not(mine))
        def _():
            send[rest % 2, rest // 2] = part


def attention_forward(
    scalars, x_ref, msg_ref, gain_ref, shift_ref, bias_ref, out_bias_ref, own, near, far,
    qkv_out, probs_out, ctx_out, s2_out, rows, normed, weight, total, *, patches, heads,
):
    slot = pl.program_id(0)
    place = scalars[1]
    frames, tokens, width = x_ref.shape
    local = heads * HS

    @pl.when(slot == 0)
    def _():
        token = lax.broadcasted_iota(jnp.int32, (tokens, 1), 0)
        for i in range(frames):
            value = x_ref[i].astype(f32)
            value = jnp.where(token == patches, msg_ref[i : i + 1, :], value)
            rows[pl.ds(i * tokens, tokens), :] = value
            base, _ = norm_stats(value)
            normed[pl.ds(i * tokens, tokens), :] = (
                base * gain_ref[...] + shift_ref[...]
            ).astype(bf16)
        total[...] = jnp.zeros_like(total)

    place_weight(weight, own, near, far, place, slot)
    projected = (nn(normed[...], weight[:, : 3 * local]) + bias_ref[...]).astype(bf16)
    qkv_out[...] = projected
    key_ok = lax.broadcasted_iota(jnp.int32, (tokens, tokens), 1) <= patches
    blank = jnp.zeros((tokens, width // 3 - local), bf16)
    for i in range(frames):
        block = projected[i * tokens : (i + 1) * tokens]
        pieces = [blank]
        for j in range(heads):
            q = block[:, j * HS : (j + 1) * HS]
            k = block[:, local + j * HS : local + (j + 1) * HS]
            v = block[:, 2 * local + j * HS : 2 * local + (j + 1) * HS]
            scores = jnp.where(key_ok, nt(q, k) * score_scale, masked_score)
            scores = jnp.exp(scores - jnp.max(scores, axis=-1, keepdims=True))
            probs = (scores / jnp.sum(scores, axis=-1, keepdims=True)).astype(bf16)
            probs_out[i * heads + j] = probs
            pieces.append(nn(probs, v).astype(bf16))
        context = jnp.concatenate(pieces, axis=1)
        ctx_out[pl.ds(i * tokens, tokens), :] = context
        total[pl.ds(i * tokens, tokens), :] += nt(context, weight[:, 2 * width // 3 :])

    @pl.when(slot == pl.num_programs(0) - 1)
    def _():
        s2_out[...] = rows[...] + total[...] + out_bias_ref[...]


def mlp_forward(
    scalars, s2_ref, gain_ref, shift_ref, fc_bias_ref, proj_bias_ref,
    fc_own, fc_near, fc_far, proj_own, proj_near, proj_far,
    pre_out, s3_out, cls_out, normed, fc, proj, total, *, tokens, patches,
):
    slot = pl.program_id(0)
    place = scalars[1]

    @pl.when(slot == 0)
    def _():
        base, _ = norm_stats(s2_ref[...])
        normed[...] = (base * gain_ref[...] + shift_ref[...]).astype(bf16)
        total[...] = jnp.zeros_like(total)

    place_weight(fc, fc_own, fc_near, fc_far, place, slot)
    place_weight(proj, proj_own, proj_near, proj_far, place, slot)
    pre = nn(normed[...], fc[...]) + fc_bias_ref[...]
    pre_out[...] = pre
    hidden = (pre * jax.nn.sigmoid(gelu_rate * pre)).astype(bf16)
    total[...] += nn(hidden, proj[...])

    @pl.when(slot == pl.num_programs(0) - 1)
    def _():
        final = s2_ref[...] + total[...] + proj_bias_ref[...]
        for i in range(s3_out.shape[0]):
            s3_out[i] = final[i * tokens : (i + 1) * tokens].astype(bf16)
            cls_out[i : i + 1, :] = final[i * tokens : i * tokens + 1]


def mlp_backward(
    scalars, up_ref, cls_ref, s2_ref, pre_ref, gain_ref, shift_ref,
    fc_own, fc_near, fc_far, proj_own, proj_near, proj_far,
    fc_keep, fc_send, proj_keep, proj_send, fc_bias_out, vec_out, g2_out,
    normed, grad3, fc, proj, total,
):
    slot = pl.program_id(0)
    place = scalars[1]
    frames, tokens, width = up_ref.shape

    @pl.when(slot == 0)
    def _():
        base, _ = norm_stats(s2_ref[...])
        normed[...] = (base * gain_ref[...] + shift_ref[...]).astype(bf16)
        token = lax.broadcasted_iota(jnp.int32, (tokens, 1), 0)
        for i in range(frames):
            value = up_ref[i].astype(f32)
            value = value + jnp.where(token == 0, cls_ref[i : i + 1, :], 0.0)
            grad3[pl.ds(i * tokens, tokens), :] = value
        total[...] = jnp.zeros_like(total)

    place_weight(fc, fc_own, fc_near, fc_far, place, slot)
    place_weight(proj, proj_own, proj_near, proj_far, place, slot)
    mlp_grad = grad3[...].astype(bf16)
    pre = pre_ref[...]
    gate = jax.nn.sigmoid(gelu_rate * pre)
    hidden = (pre * gate).astype(bf16)
    spread_grad(proj_keep, proj_send, tn(hidden, mlp_grad), place)
    hidden_grad = nt(mlp_grad, proj[...])
    pre_grad = (hidden_grad * (gate + gelu_rate * pre * gate * (1.0 - gate))).astype(bf16)
    fc_bias_out[...] = jnp.sum(pre_grad.astype(f32), axis=0, keepdims=True)
    spread_grad(fc_keep, fc_send, tn(normed[...], pre_grad), place)
    total[...] += nt(pre_grad, fc[...])

    @pl.when(slot == pl.num_programs(0) - 1)
    def _():
        base, factor = norm_stats(s2_ref[...])
        grad_in, gain_grad, shift_grad = norm_back(total[...], base, factor, gain_ref[...])
        g2_out[...] = grad3[...] + grad_in
        vec_out[0:1, :] = gain_grad
        vec_out[1:2, :] = shift_grad
        vec_out[2:3, :] = jnp.sum(grad3[...].astype(bf16).astype(f32), axis=0, keepdims=True)
        vec_out[3:8, :] = jnp.zeros((5, width), f32)


def attention_backward(
    scalars, g2_ref, x_ref, msg_ref, qkv_ref, probs_ref, ctx_ref, gain_ref, shift_ref,
    own, near, far,
    keep, send, bias_out, vec_out, g1_out,
    normed, grad, dproj, weight, total, *, patches, heads,
):
    slot = pl.program_id(0)
    place = scalars[1]
    frames, tokens, width = x_ref.shape
    local = heads * HS
    wide = width // 3
    token = lax.broadcasted_iota(jnp.int32, (tokens, 1), 0)

    def stream(i):
        return jnp.where(token == patches, msg_ref[i : i + 1, :], x_ref[i].astype(f32))

    @pl.when(slot == 0)
    def _():
        for i in range(frames):
            base, _ = norm_stats(stream(i))
            normed[pl.ds(i * tokens, tokens), :] = (
                base * gain_ref[...] + shift_ref[...]
            ).astype(bf16)
        grad[...] = g2_ref[...].astype(bf16)
        total[...] = jnp.zeros_like(total)

    place_weight(weight, own, near, far, place, slot)
    context_grad = nn(grad[...], weight[:, 2 * wide :]).astype(bf16)
    skip = wide - local
    for i in range(frames):
        span = slice(i * tokens, (i + 1) * tokens)
        dq, dk, dv = [], [], []
        for j in range(heads):
            q = qkv_ref[span, j * HS : (j + 1) * HS]
            k = qkv_ref[span, local + j * HS : local + (j + 1) * HS]
            v = qkv_ref[span, 2 * local + j * HS : 2 * local + (j + 1) * HS]
            cg = context_grad[span, skip + j * HS : skip + (j + 1) * HS]
            low = probs_ref[i * heads + j]
            probs = low.astype(f32)
            prob_grad = nt(cg, v)
            weighted = probs * prob_grad
            score_grad = (
                weighted - probs * jnp.sum(weighted, axis=-1, keepdims=True)
            ).astype(bf16)
            dq.append((nn(score_grad, k) * score_scale).astype(bf16))
            dk.append((tn(score_grad, q) * score_scale).astype(bf16))
            dv.append(tn(low, cg).astype(bf16))
        dproj[pl.ds(i * tokens, tokens), :] = jnp.concatenate(
            dq + dk + dv + [jnp.zeros((tokens, width - 3 * local), bf16)], axis=1
        )
    all_grads = dproj[...]
    bias_out[...] = jnp.sum(all_grads.astype(f32), axis=0, keepdims=True)
    low_part = tn(normed[...], all_grads[:, : 2 * wide])
    high_part = tn(normed[...], all_grads[:, 2 * wide :]) + tn(grad[...], ctx_ref[...])
    spread_grad(keep, send, jnp.concatenate([low_part, high_part], axis=1), place)
    total[...] += nt(all_grads[:, : 3 * local], weight[:, : 3 * local])

    @pl.when(slot == pl.num_programs(0) - 1)
    def _():
        gain_total = jnp.zeros((1, width), f32)
        shift_total = jnp.zeros((1, width), f32)
        for i in range(frames):
            span = pl.ds(i * tokens, tokens)
            base, factor = norm_stats(stream(i))
            grad_in, gain_grad, shift_grad = norm_back(
                total[span, :], base, factor, gain_ref[...]
            )
            g1_out[i] = grad_in + g2_ref[span, :]
            gain_total = gain_total + gain_grad
            shift_total = shift_total + shift_grad
        vec_out[0:1, :] = gain_total
        vec_out[1:2, :] = shift_total
        vec_out[2:3, :] = jnp.sum(grad[...].astype(f32), axis=0, keepdims=True)
        vec_out[3:8, :] = jnp.zeros((5, width), f32)


def whole(array):
    count = array.ndim
    return pl.BlockSpec(array.shape, lambda s, sc: (0,) * count)


def per_slot(array):
    count = array.ndim - 1
    return pl.BlockSpec((None,) + array.shape[1:], lambda s, sc: (s,) + (0,) * count)


def weight_specs(own, near, far, which):
    def pick(s, sc):
        return (0, 0, jnp.maximum(s - 1, 0), which, 0, 0)

    far_spec = pl.BlockSpec((2, 4, None, None) + near.shape[4:], pick)
    return [pl.BlockSpec(own.shape, lambda s, sc: (0, 0)), far_spec, far_spec]


def call(kernel, scalars, inputs, specs, outs, scratch, slots, flops):
    shapes, out_specs = zip(*outs)
    moved = sum(a.size * a.dtype.itemsize for a in inputs)
    return pl.pallas_call(
        kernel,
        grid_spec=pltpu.PrefetchScalarGridSpec(
            num_scalar_prefetch=1,
            grid=(slots,),
            in_specs=specs,
            out_specs=list(out_specs),
            scratch_shapes=scratch,
        ),
        out_shape=list(shapes),
        cost_estimate=pl.CostEstimate(flops=flops, bytes_accessed=moved, transcendentals=0),
    )(scalars, *inputs)


def shaped(shape, dtype):
    return jax.ShapeDtypeStruct(shape, dtype)


def slot_out(shape, dtype, slots):
    count = len(shape)
    return (
        shaped((slots,) + tuple(shape), dtype),
        pl.BlockSpec((None,) + tuple(shape), lambda s, sc: (s,) + (0,) * count),
    )


def full_out(shape, dtype):
    count = len(shape)
    return shaped(tuple(shape), dtype), pl.BlockSpec(tuple(shape), lambda s, sc: (0,) * count)


def gather_weights(matrices, place):
    block = matrices[0].shape[0] // GROUP
    half = block // 2
    mine = jnp.stack(
        [lax.dynamic_slice_in_dim(m, place * block, block, axis=0) for m in matrices]
    )
    count = lax.axis_size("heads")
    got = [to_heads(mine, step) for step in range(1, count)]
    first = jnp.stack([g[:, :half] for g in got])
    second = jnp.stack([g[:, half:] for g in got])
    first = jnp.stack([first, swap_frames(first, 2)])
    second = jnp.stack([second, swap_frames(second, 4)])
    first_far = swap_frames(first, 4)
    second_far = swap_frames(second, 2)
    near = jnp.stack(
        [
            jnp.concatenate([first, first_far], axis=0),
            jnp.concatenate([second, second_far], axis=0),
        ]
    )
    return near, swap_frames(near, 1)


def reduce_grads(keep, send):
    half = keep.shape[4] // 2
    got = swap_frames(send, 1)

    def summed(x, y, low):
        rows = slice(0, half) if low else slice(half, 2 * half)
        index = (slice(None), slice(None), x, y, rows)
        return keep[index].astype(f32) + got[index].astype(f32)

    both = slice(None)
    first_got = swap_frames(summed(1, both, True).astype(bf16), 2)
    second_got = swap_frames(summed(both, 1, False).astype(bf16), 4)

    def next_first(y):
        return summed(0, y, True) + first_got[:, :, y].astype(f32)

    def next_second(x):
        return summed(x, 0, False) + second_got[:, :, x].astype(f32)

    first_last = swap_frames(next_first(1).astype(bf16), 4)
    second_last = swap_frames(next_second(1).astype(bf16), 2)
    first = next_first(0) + first_last.astype(f32)
    second = next_second(0) + second_last.astype(f32)
    total = jnp.concatenate([first, second], axis=2).astype(bf16)
    for bit in frame_bits(GROUP):
        total = (total.astype(f32) + swap_frames(total, bit).astype(f32)).astype(bf16)
    own = total[0].astype(f32)
    for step in range(1, total.shape[0]):
        own = own + to_heads(total[step], -step).astype(f32)
    return own.astype(bf16)


def regather(rows, place):
    half = rows.shape[1] // 2
    first, second = rows[:, :half], rows[:, half:]
    first = jnp.stack([first, swap_frames(first, 2)])
    second = jnp.stack([second, swap_frames(second, 4)])
    first = jnp.concatenate([first, swap_frames(first, 4)], axis=0)
    second = jnp.concatenate([second, swap_frames(second, 2)], axis=0)
    second = jnp.stack([second[0], second[2], second[1], second[3]])
    near = jnp.concatenate([first, second], axis=2)
    both = jnp.stack([near, swap_frames(near, 1)], axis=1)
    both = both.reshape((GROUP,) + rows.shape)
    order = jnp.arange(GROUP) ^ place
    both = both[order]
    return jnp.moveaxis(both, 0, 1).reshape(rows.shape[0], GROUP * rows.shape[1], rows.shape[2])


def contrast_loss(pooled_sum, frame_counts, group_ids):
    video_count = group_ids.shape[0]
    pooled = pooled_sum / frame_counts[:, None]
    unit = pooled * lax.rsqrt(jnp.sum(pooled * pooled, axis=1, keepdims=True) + 1e-06)
    logits = jnp.matmul(unit, unit.T, precision=exact) / contrast_sharpness
    video_list = jnp.arange(video_count, dtype=jnp.int32)
    itself = video_list[:, None] == video_list[None, :]
    logits = jnp.where(itself, masked_score, logits)
    log_total = jax.nn.logsumexp(logits, axis=1)
    positive = jnp.logical_and(
        group_ids[:, None] == group_ids[None, :], jnp.logical_not(itself)
    ).astype(f32)
    pos_count = jnp.maximum(jnp.sum(positive, axis=1), 1.0)
    per_anchor = jnp.sum(positive * (log_total[:, None] - logits), axis=1) / pos_count
    return jnp.sum(per_anchor)


def on_device(
    frames_in,
    upstream,
    video_of_frame,
    group_ids,
    msg_fc_weight,
    msg_fc_bias,
    msg_gain,
    msg_shift,
    msg_qkv_weight,
    msg_qv_bias,
    courier_result_kernel,
    msg_out_bias,
    ln1_gain,
    ln1_shift,
    qkv_weight,
    qv_bias,
    picture_result_kernel,
    out_bias,
    ln2_gain,
    ln2_shift,
    fc_weight,
    fc_bias,
    proj_weight,
    proj_bias,
):
    block_frames, patches, local = frames_in.shape
    width = msg_qkv_weight.shape[0]
    slots = lax.axis_size("heads")
    own_frames = block_frames // slots
    heads = local // HS
    tokens = -(-(patches + 1) // 16) * 16
    rows = own_frames * tokens
    frame_index = lax.axis_index("frames")
    head_index = lax.axis_index("heads")
    place = frame_index % GROUP
    scalars = jnp.stack([head_index, place]).astype(jnp.int32)
    steps = range(1, slots)

    def frames_of(array, step):
        start = jnp.mod(head_index + step, slots) * own_frames
        return lax.dynamic_slice_in_dim(array, start, own_frames, axis=0)

    def to_rows(array):
        parts = [frames_of(array, 0)] + [to_heads(frames_of(array, s), s) for s in steps]
        value = jnp.concatenate(in_order(parts, head_index), axis=2)
        return jnp.pad(value, ((0, 0), (0, tokens - patches), (0, 0)))

    def features_of(array, step):
        start = jnp.mod(head_index + step, slots) * local
        return lax.dynamic_slice_in_dim(array, start, local, axis=array.ndim - 1)

    def to_features(array):
        parts = [features_of(array, 0)] + [to_heads(features_of(array, s), s) for s in steps]
        return jnp.concatenate(in_order(parts, head_index), axis=0)

    def heads_rows(value):
        parts = [value] + [to_heads(value, s) for s in steps]
        return jnp.concatenate(in_order(parts, head_index), axis=0)

    cls_own = frames_in[:, 0, :]
    vectors = jnp.stack(
        [
            msg_fc_bias, msg_gain, msg_shift, msg_out_bias, ln1_gain, ln1_shift,
            out_bias, ln2_gain, ln2_shift, proj_bias,
        ]
    )
    vectors = jnp.concatenate([vectors, qv_bias, fc_bias.reshape(slots, local)], axis=0)
    vectors = vectors.astype(f32)
    start_part = nn(cls_own, msg_fc_weight)
    small = jnp.concatenate([start_part, vectors.reshape(-1, width)], axis=0)
    small = [small] + [to_heads(small, s) for s in steps]
    vector_slots = [part[block_frames:].reshape(-1, local) for part in small]
    natural = jnp.concatenate(in_order([v[:10] for v in vector_slots], head_index), axis=1)
    (
        msg_fc_full, msg_gain_full, msg_shift_full, msg_out_full, ln1_gain_full, ln1_shift_full,
        out_full, ln2_gain_full, ln2_shift_full, proj_full,
    ) = [natural[i : i + 1] for i in range(10)]
    zero_bias = jnp.zeros((local,), f32)
    qkv_bias = jnp.stack(
        [jnp.concatenate([v[10], zero_bias, v[11]])[None] for v in vector_slots]
    )
    fc_bias_slots = jnp.stack([v[12:].reshape(1, -1) for v in vector_slots])
    start_block = sum(part[:block_frames] for part in small) + msg_fc_full

    x = to_rows(frames_in)

    out_turned = picture_result_kernel.T
    attn_own = jnp.concatenate([qkv_weight.reshape(width, 3 * local), out_turned], axis=1)
    attn_near, attn_far = gather_weights([attn_own], place)

    sent = jnp.concatenate(
        [start_block, cls_own.astype(f32), jnp.zeros((block_frames, 64), f32)], axis=1
    )
    sent = all_frames(sent)
    start = sent[:, :width]
    cls_all = sent[:, width : width + local].astype(bf16)
    frame_total = start.shape[0]
    places = frame_index ^ jnp.arange(lax.axis_size("frames"))
    near_ids = video_of_frame.reshape(-1, block_frames)[places].reshape(-1)
    msg_base, msg_factor = norm_stats(start)
    msg_rows = (msg_base * msg_gain_full + msg_shift_full).astype(bf16)
    msg_flat = msg_qkv_weight.reshape(width, 3 * local)
    msg_bias = jnp.concatenate([msg_qv_bias[0].astype(f32), zero_bias, msg_qv_bias[1].astype(f32)])
    msg_proj = (nn(msg_rows, msg_flat) + msg_bias).astype(bf16)
    msg_split = msg_proj.reshape(frame_total, 3, heads, HS)
    msg_q, msg_k, msg_v = msg_split[:, 0], msg_split[:, 1], msg_split[:, 2]
    same = (near_ids[:, None] == near_ids[None, :])[None]
    msg_scores = jnp.einsum("qhd,khd->hqk", msg_q, msg_k, preferred_element_type=f32) * score_scale
    msg_probs = jax.nn.softmax(jnp.where(same, msg_scores, masked_score), axis=-1)
    msg_low = msg_probs.astype(bf16)
    msg_context = jnp.einsum("hqk,khd->qhd", msg_low, msg_v, preferred_element_type=f32)
    msg_context = msg_context.astype(bf16).reshape(frame_total, local)
    msg_part = nn(msg_context[:block_frames], courier_result_kernel)
    msg_sum = frames_of(msg_part, 0) + sum(to_heads(frames_of(msg_part, s), s) for s in steps)
    message = frames_of(start_block, 0) + msg_sum + msg_out_full

    pad_tail = width // 3 - local
    outs = call(
        functools.partial(attention_forward, patches=patches, heads=heads),
        scalars,
        [x, message, ln1_gain_full, ln1_shift_full, qkv_bias, out_full, attn_own, attn_near, attn_far],
        [whole(x), whole(message), whole(ln1_gain_full), whole(ln1_shift_full), per_slot(qkv_bias),
         whole(out_full)] + weight_specs(attn_own, attn_near, attn_far, 0),
        [
            slot_out((rows, 3 * local), bf16, slots),
            slot_out((own_frames * heads, tokens, tokens), bf16, slots),
            slot_out((rows, local + pad_tail), bf16, slots),
            full_out((rows, width), f32),
        ],
        [
            pltpu.VMEM((rows, width), f32),
            pltpu.VMEM((rows, width), bf16),
            pltpu.VMEM((width, width), bf16),
            pltpu.VMEM((rows, width), f32),
        ],
        slots,
        2 * rows * width * width * slots,
    )
    qkv, probs, context, stream_two = outs

    mlp_near, mlp_far = gather_weights([fc_weight, proj_weight], place)
    up = to_rows(upstream)

    mlp_specs = weight_specs(fc_weight, mlp_near, mlp_far, 0) + weight_specs(
        proj_weight, mlp_near, mlp_far, 1
    )
    mlp_weights = [fc_weight, mlp_near, mlp_far, proj_weight, mlp_near, mlp_far]
    hidden_local = fc_weight.shape[1]
    pre, stream_three, cls_three = call(
        functools.partial(mlp_forward, tokens=tokens, patches=patches),
        scalars,
        [stream_two, ln2_gain_full, ln2_shift_full, fc_bias_slots, proj_full] + mlp_weights,
        [whole(stream_two), whole(ln2_gain_full), whole(ln2_shift_full), per_slot(fc_bias_slots),
         whole(proj_full)] + mlp_specs,
        [
            slot_out((rows, hidden_local), f32, slots),
            full_out((own_frames, tokens, width), bf16),
            full_out((own_frames, width), f32),
        ],
        [
            pltpu.VMEM((rows, width), bf16),
            pltpu.VMEM((width, hidden_local), bf16),
            pltpu.VMEM((hidden_local, width), bf16),
            pltpu.VMEM((rows, width), f32),
        ],
        slots,
        4 * rows * width * hidden_local * slots,
    )
    output = to_features(stream_three[:, :patches])

    cls_block = heads_rows(cls_three)
    cls_every = all_frames(cls_block)
    video_count = group_ids.shape[0]
    video_list = jnp.arange(video_count, dtype=jnp.int32)
    onehot = (near_ids[None, :] == video_list[:, None]).astype(f32)
    frame_counts = jnp.sum(onehot, axis=1)
    pooled_sum = jnp.dot(onehot, cls_every, precision=exact)
    loss_value, loss_pull = jax.vjp(
        lambda total: contrast_loss(total, frame_counts, group_ids), pooled_sum
    )
    (pool_grad,) = loss_pull(jnp.ones((), f32))
    own_onehot = frames_of(onehot[:, :block_frames].T, 0)
    cls_grad = jnp.dot(own_onehot, pool_grad, precision=exact)

    piece = (2, 2, width // GROUP, width)
    grads = call(
        mlp_backward,
        scalars,
        [up, cls_grad, stream_two, pre, ln2_gain_full, ln2_shift_full] + mlp_weights,
        [whole(up), whole(cls_grad), whole(stream_two), per_slot(pre), whole(ln2_gain_full),
         whole(ln2_shift_full)] + mlp_specs,
        [
            slot_out(piece, bf16, slots),
            slot_out(piece, bf16, slots),
            slot_out(piece, bf16, slots),
            slot_out(piece, bf16, slots),
            slot_out((1, hidden_local), f32, slots),
            full_out((8, width), f32),
            full_out((rows, width), f32),
        ],
        [
            pltpu.VMEM((rows, width), bf16),
            pltpu.VMEM((rows, width), f32),
            pltpu.VMEM((width, hidden_local), bf16),
            pltpu.VMEM((hidden_local, width), bf16),
            pltpu.VMEM((rows, width), f32),
        ],
        slots,
        8 * rows * width * hidden_local * slots,
    )
    fc_keep, fc_send, proj_keep, proj_send, fc_bias_grad, mlp_vec, grad_two = grads
    mlp_grads = regather(
        reduce_grads(
            jnp.stack([fc_keep, proj_keep], axis=1), jnp.stack([fc_send, proj_send], axis=1)
        ),
        place,
    )

    grads = call(
        functools.partial(attention_backward, patches=patches, heads=heads),
        scalars,
        [grad_two, x, message, qkv, probs, context, ln1_gain_full, ln1_shift_full, attn_own, attn_near,
         attn_far],
        [whole(grad_two), whole(x), whole(message), per_slot(qkv), per_slot(probs), per_slot(context),
         whole(ln1_gain_full), whole(ln1_shift_full)]
        + weight_specs(attn_own, attn_near, attn_far, 0),
        [
            slot_out(piece, bf16, slots),
            slot_out(piece, bf16, slots),
            slot_out((1, width), f32, slots),
            full_out((8, width), f32),
            full_out((own_frames, tokens, width), f32),
        ],
        [
            pltpu.VMEM((rows, width), bf16),
            pltpu.VMEM((rows, width), bf16),
            pltpu.VMEM((rows, width), bf16),
            pltpu.VMEM((width, width), bf16),
            pltpu.VMEM((rows, width), f32),
        ],
        slots,
        6 * rows * width * width * slots,
    )
    attn_keep, attn_send, proj_bias_grad, attn_vec, grad_one = grads
    attn_grads = regather(reduce_grads(attn_keep[:, None], attn_send[:, None]), place)
    grad_features = to_features(grad_one[:, :patches].astype(bf16)).astype(f32)

    grad_message = all_frames(heads_rows(grad_one[:, patches]))
    msg_attn_grad = grad_message.astype(bf16)
    msg_bias_sum = jnp.sum(msg_attn_grad.astype(f32), axis=0)
    grad_msg_out_bias = features_of(msg_bias_sum, 0)
    grad_msg_out_weight = tn(msg_context, msg_attn_grad)
    msg_context_grad = nt(msg_attn_grad, courier_result_kernel).astype(bf16)
    msg_context_grad = msg_context_grad.reshape(frame_total, heads, HS)
    msg_prob_grad = jnp.einsum("qhd,khd->hqk", msg_context_grad, msg_v, preferred_element_type=f32)
    msg_score_grad = msg_probs * (
        msg_prob_grad - jnp.sum(msg_probs * msg_prob_grad, axis=-1, keepdims=True)
    )
    msg_score_grad = msg_score_grad.astype(bf16)
    msg_dq = jnp.einsum("hqk,khd->qhd", msg_score_grad, msg_k, preferred_element_type=f32)
    msg_dk = jnp.einsum("hqk,qhd->khd", msg_score_grad, msg_q, preferred_element_type=f32)
    msg_dv = jnp.einsum("hqk,qhd->khd", msg_low, msg_context_grad, preferred_element_type=f32)
    msg_grads = jnp.stack([msg_dq * score_scale, msg_dk * score_scale, msg_dv], axis=1)
    msg_grads = msg_grads.astype(bf16).reshape(frame_total, 3 * local)
    grad_msg_qkv_weight = tn(msg_rows, msg_grads).reshape(width, 3, local)
    msg_totals = jnp.sum(msg_grads.astype(f32), axis=0).reshape(3, local)
    grad_msg_qv_bias = jnp.stack([msg_totals[0], msg_totals[2]])
    back_part = nt(msg_grads, msg_flat)
    back = back_part + sum(to_heads(back_part.astype(bf16), s).astype(f32) for s in steps)
    msg_norm_in, msg_gain_grad, msg_shift_grad = norm_back(
        back, msg_base, msg_factor, msg_gain_full
    )
    grad_msg_gain = features_of(msg_gain_grad[0], 0)
    grad_msg_shift = features_of(msg_shift_grad[0], 0)
    start_grad = (grad_message + msg_norm_in).astype(bf16)
    grad_msg_fc_bias = features_of(jnp.sum(start_grad.astype(f32), axis=0), 0)
    grad_msg_fc_weight = tn(cls_all, start_grad)
    cls_back = nt(start_grad[:block_frames], msg_fc_weight)
    grad_input = grad_features.at[:, 0, :].add(cls_back)

    feature_rows = jnp.concatenate([attn_vec[:3], mlp_vec[:3]], axis=0)
    per_head = [
        jnp.concatenate(
            [
                features_of(feature_rows, -s),
                proj_bias_grad[s, 0, :local][None],
                proj_bias_grad[s, 0, 2 * local : 3 * local][None],
                fc_bias_grad[s].reshape(slots, local),
            ],
            axis=0,
        ).reshape(-1, width)
        for s in range(slots)
    ]
    vec = per_head[0] + sum(to_heads(per_head[s], -s) for s in steps)
    for bit in frame_bits():
        vec = vec + swap_frames(vec, bit)
    vec = vec.reshape(-1, local)

    attn_final = attn_grads[0].astype(f32)
    return (
        output,
        loss_value,
        grad_input,
        grad_msg_fc_weight,
        grad_msg_fc_bias,
        grad_msg_gain,
        grad_msg_shift,
        grad_msg_qkv_weight,
        grad_msg_qv_bias,
        grad_msg_out_weight,
        grad_msg_out_bias,
        vec[0],
        vec[1],
        attn_final[:, : 3 * local].reshape(width, 3, local),
        vec[6:8],
        attn_final[:, 3 * local :].T,
        vec[2],
        vec[3],
        vec[4],
        mlp_grads[0].astype(f32),
        vec[8:].reshape(-1),
        mlp_grads[1].astype(f32),
        vec[5],
    )


def solution(mesh):
    placed = (
        P("frames", None, "heads"),
        P("frames", None, "heads"),
        P(),
        P(),
        P("heads", None),
        P("heads"),
        P("heads"),
        P("heads"),
        P(None, None, "heads"),
        P(None, "heads"),
        P("heads", None),
        P("heads"),
        P("heads"),
        P("heads"),
        P(None, None, "heads"),
        P(None, "heads"),
        P("heads", None),
        P("heads"),
        P("heads"),
        P("heads"),
        P(None, "heads"),
        P("heads"),
        P("heads", None),
        P("heads"),
    )
    return jax.shard_map(
        on_device,
        mesh=mesh,
        in_specs=placed,
        out_specs=(
            P("frames", None, "heads"),
            P(),
            P("frames", None, "heads"),
            P("heads", None),
            P("heads"),
            P("heads"),
            P("heads"),
            P(None, None, "heads"),
            P(None, "heads"),
            P("heads", None),
            P("heads"),
            P("heads"),
            P("heads"),
            P(None, None, "heads"),
            P(None, "heads"),
            P("heads", None),
            P("heads"),
            P("heads"),
            P("heads"),
            P(None, "heads"),
            P("heads"),
            P("heads", None),
            P("heads"),
        ),
        check_vma=False,
    )
```

```python
import functools

import jax
import jax.numpy as jnp
from jax import lax
from jax.experimental import pallas as pl
from jax.experimental.pallas import tpu as pltpu
from jax.sharding import PartitionSpec as P

HS = 64
GROUP = 8

norm_eps = 1e-05
score_scale = 0.125
gelu_rate = 1.702
contrast_sharpness = 0.02
masked_score = -1000000000.0
exact = lax.Precision.HIGHEST
f32 = jnp.float32
bf16 = jnp.bfloat16

PIECES = ((0, 2, 4, 6), (0, 4, 2, 6))


def nn(left, right):
    return lax.dot_general(left, right, (((1,), (0,)), ((), ())), preferred_element_type=f32)


def nt(left, right):
    return lax.dot_general(left, right, (((1,), (1,)), ((), ())), preferred_element_type=f32)


def tn(left, right):
    return lax.dot_general(left, right, (((0,), (0,)), ((), ())), preferred_element_type=f32)


def to_heads(value, step):
    count = lax.axis_size("heads")
    return lax.ppermute(value, "heads", [(i, (i + step) % count) for i in range(count)])


def swap_frames(value, bit):
    count = lax.axis_size("frames")
    return lax.ppermute(value, "frames", [(i, i ^ bit) for i in range(count)])


def frame_bits(start=1):
    count = lax.axis_size("frames")
    bits = []
    bit = start
    while bit < count:
        bits.append(bit)
        bit *= 2
    return bits


def norm_stats(rows):
    center = jnp.mean(rows, axis=-1, keepdims=True)
    offset = rows - center
    factor = lax.rsqrt(jnp.mean(offset * offset, axis=-1, keepdims=True) + norm_eps)
    return offset * factor, factor


def norm_back(grad_out, normed, factor, gain):
    scaled = grad_out * gain
    first = jnp.mean(scaled, axis=-1, keepdims=True)
    second = jnp.mean(scaled * normed, axis=-1, keepdims=True)
    grad_in = factor * (scaled - first - normed * second)
    return (
        grad_in,
        jnp.sum(grad_out * normed, axis=0, keepdims=True),
        jnp.sum(grad_out, axis=0, keepdims=True),
    )


def place_weight(target, own, near, far, place, slot):
    block = target.shape[0] // GROUP
    half = block // 2

    @pl.when(slot == 0)
    def _():
        target[...] = own[...]

    @pl.when(slot > 0)
    def _():
        for q in range(2):
            for j in range(4):
                here = (place ^ PIECES[q][j]) * block + q * half
                there = (place ^ PIECES[q][j] ^ 1) * block + q * half
                target[pl.ds(pl.multiple_of(here, 16), half), :] = near[q, j]
                target[pl.ds(pl.multiple_of(there, 16), half), :] = far[q, j]


def spread_grad(keep, send, value, place):
    block = value.shape[0] // GROUP
    for owner in range(GROUP):
        part = value[owner * block : (owner + 1) * block].astype(bf16)
        offset = place ^ owner
        rest = offset // 2
        mine = offset % 2 == 0

        @pl.when(mine)
        def _():
            keep[rest % 2, rest // 2] = part

        @pl.when(jnp.logical_not(mine))
        def _():
            send[rest % 2, rest // 2] = part


def pick_rows(array, first, count):
    row = lax.broadcasted_iota(jnp.int32, (array.shape[0], 1), 0)
    return [
        jnp.sum(jnp.where(row == first + i, array, 0.0), axis=0, keepdims=True)
        for i in range(count)
    ]


def put_rows(rows, first, total):
    row = lax.broadcasted_iota(jnp.int32, (total, 1), 0)
    value = jnp.zeros((total, rows[0].shape[1]), f32)
    for i, line in enumerate(rows):
        value = jnp.where(row == first + i, line, value)
    return value


def join_features(pieces, i, head_index):
    values = [piece[i] for piece in pieces]
    count = len(values)
    blocks = []
    for block in range(count):
        value = values[0]
        slot = (head_index - block + count) % count
        for s in range(1, count):
            value = jnp.where(slot == s, values[s], value)
        blocks.append(value)
    return jnp.concatenate(blocks, axis=1)


def split_features(value, pieces, i, head_index):
    count = len(pieces)
    local = value.shape[1] // count
    blocks = [value[:, b * local : (b + 1) * local] for b in range(count)]
    for s, piece in enumerate(pieces):
        block = (head_index + s) % count
        part = blocks[0]
        for b in range(1, count):
            part = jnp.where(block == b, blocks[b], part)
        piece[i] = part


def message_forward(
    p0, p1, p2, p3, ids_col, ids_row, nat, weight, bias, courier,
    start_out, cls_out, rows_out, proj_out, probs_out, ctx_out, part_out, *, heads, block,
):
    width = nat.shape[1]
    local = heads * HS
    each = p0.shape[0]
    for j, piece in enumerate((p0, p1, p2, p3)):
        span = pl.ds(j * each, each)
        start_out[span, :] = piece[:, :width] + nat[block : block + 1, :]
        cls_out[span, :] = piece[:, width : width + local].astype(bf16)
    base, _ = norm_stats(start_out[...])
    rows = (base * nat[block + 1 : block + 2, :] + nat[block + 2 : block + 3, :]).astype(bf16)
    rows_out[...] = rows
    proj = [
        (nn(rows, weight[:, c, :]) + bias[:, c * local : (c + 1) * local]).astype(bf16)
        for c in range(3)
    ]
    proj_out[...] = jnp.concatenate(proj, axis=1)
    same = ids_col[...] == ids_row[...]
    context = []
    for j in range(heads):
        q, k, v = [p[:, j * HS : (j + 1) * HS] for p in proj]
        scores = jnp.where(same, nt(q, k) * score_scale, masked_score)
        scores = jnp.exp(scores - jnp.max(scores, axis=-1, keepdims=True))
        probs = scores / jnp.sum(scores, axis=-1, keepdims=True)
        probs_out[j] = probs
        context.append(nn(probs.astype(bf16), v).astype(bf16))
    context = jnp.concatenate(context, axis=1)
    ctx_out[...] = context
    part_out[...] = nn(context[:16], courier[...])[:block]


def message_back_one(
    p0, p1, p2, p3, rows, proj, probs_ref, ctx, weight, courier,
    grad_out, weight_out, courier_out, back_out, send_out, bias_out, sums_out, *, heads,
):
    local = heads * HS
    each = p0.shape[0]
    for j, piece in enumerate((p0, p1, p2, p3)):
        grad_out[pl.ds(j * each, each), :] = piece[...]
    grad = grad_out[...].astype(bf16)
    bias_out[...] = jnp.sum(grad.astype(f32), axis=0, keepdims=True)
    courier_out[...] = tn(ctx[...], grad)
    context_grad = nt(grad, courier[...]).astype(bf16)
    dq, dk, dv = [], [], []
    for j in range(heads):
        q, k, v = [
            proj[:, c * local + j * HS : c * local + (j + 1) * HS] for c in range(3)
        ]
        cg = context_grad[:, j * HS : (j + 1) * HS]
        probs = probs_ref[j]
        weighted = probs * nt(cg, v)
        score_grad = (weighted - probs * jnp.sum(weighted, axis=-1, keepdims=True)).astype(bf16)
        dq.append((nn(score_grad, k) * score_scale).astype(bf16))
        dk.append((tn(score_grad, q) * score_scale).astype(bf16))
        dv.append(tn(probs.astype(bf16), cg).astype(bf16))
    back = None
    for c, parts in enumerate((dq, dk, dv)):
        value = jnp.concatenate(parts, axis=1)
        weight_out[:, c, :] = tn(rows[...], value)
        sums_out[c : c + 1, :] = jnp.sum(value.astype(f32), axis=0, keepdims=True)
        term = nt(value, weight[:, c, :])
        back = term if back is None else back + term
    back_out[...] = back
    send_out[...] = back.astype(bf16)


def message_back_two(
    own, r1, r2, r3, grad, start, cls, nat, weight, weight_out, vec_out, cls_back_out, *, block
):
    total = own[...]
    for piece in (r1, r2, r3):
        total = total + piece[...].astype(f32)
    base, factor = norm_stats(start[...])
    grad_in, gain_grad, shift_grad = norm_back(total, base, factor, nat[block + 1 : block + 2, :])
    start_grad = (grad[...] + grad_in).astype(bf16)
    weight_out[...] = tn(cls[...], start_grad)
    vec_out[0:1, :] = gain_grad
    vec_out[1:2, :] = shift_grad
    vec_out[2:3, :] = jnp.sum(start_grad.astype(f32), axis=0, keepdims=True)
    cls_back_out[...] = nt(start_grad[:16], weight[...])[:block]


def contrast(
    p0, p1, p2, p3, ids_row, ids_col, group_col, group_row, loss_out, grad_out, *, videos, block
):
    each = p0.shape[0]
    padded = group_col.shape[0]
    video = lax.broadcasted_iota(jnp.int32, (padded, 1), 0)
    onehot = (ids_row[...] == video).astype(f32)
    counts = jnp.sum(onehot, axis=1, keepdims=True)
    counts = jnp.where(video < videos, counts, 1.0)
    pooled = None
    for j, piece in enumerate((p0, p1, p2, p3)):
        hot = (ids_row[:, j * each : (j + 1) * each] == video).astype(f32)
        term = jnp.dot(hot, piece[...], precision=exact, preferred_element_type=f32)
        pooled = term if pooled is None else pooled + term
    pooled = pooled / counts
    scale = lax.rsqrt(jnp.sum(pooled * pooled, axis=1, keepdims=True) + 1e-06)
    unit = pooled * scale
    logits = (
        lax.dot_general(
            unit, unit, (((1,), (1,)), ((), ())), precision=exact, preferred_element_type=f32
        )
        / contrast_sharpness
    )
    other = lax.broadcasted_iota(jnp.int32, (padded, padded), 1)
    this = lax.broadcasted_iota(jnp.int32, (padded, padded), 0)
    usable = jnp.logical_and(other != this, other < videos)
    logits = jnp.where(usable, logits, masked_score)
    top = jnp.max(logits, axis=1, keepdims=True)
    powers = jnp.exp(logits - top)
    total = jnp.sum(powers, axis=1, keepdims=True)
    log_total = top + jnp.log(total)
    real = jnp.logical_and(usable, this < videos)
    positive = jnp.where(
        jnp.logical_and(group_col[...] == group_row[...], real), 1.0, 0.0
    )
    weights = positive / jnp.maximum(jnp.sum(positive, axis=1, keepdims=True), 1.0)
    each_loss = jnp.where(real, weights * (log_total - logits), 0.0)
    loss_out[...] = jnp.sum(jnp.sum(each_loss, axis=1, keepdims=True), axis=0, keepdims=True)
    g_logits = jnp.sum(weights, axis=1, keepdims=True) * (powers / total) - weights
    g_logits = jnp.where(real, g_logits, 0.0)
    g_unit = jnp.dot(g_logits, unit, precision=exact, preferred_element_type=f32)
    g_unit = g_unit + lax.dot_general(
        g_logits, unit, (((0,), (0,)), ((), ())), precision=exact, preferred_element_type=f32
    )
    g_unit = g_unit / contrast_sharpness
    inner = jnp.sum(pooled * g_unit, axis=1, keepdims=True)
    g_pooled = scale * g_unit - scale * scale * scale * inner * pooled
    hot = (ids_col[:block, :] == lax.broadcasted_iota(jnp.int32, (block, padded), 1)).astype(f32)
    grad_out[...] = jnp.dot(hot, g_pooled / counts, precision=exact, preferred_element_type=f32)


def attention_forward(
    scalars, x0, x1, x2, x3, m0, m1, m2, m3, start, nat, bias_ref, own, near, far,
    qkv_out, probs_out, ctx_out, rows, normed, s2_out, weight, total, *, heads, block, tokens,
):
    slot = pl.program_id(0)
    head_index, place = scalars[0], scalars[1]
    frames, patches, _ = x0.shape
    width = nat.shape[1]
    local = heads * HS

    @pl.when(slot == 0)
    def _():
        lines = start[...] + m0[...] + m1[...] + m2[...] + m3[...] + nat[block + 3 : block + 4, :]
        message = pick_rows(lines, head_index * frames, frames)
        for i in range(frames):
            base = i * tokens
            rows[base : base + patches, :] = join_features((x0, x1, x2, x3), i, head_index).astype(f32)
            rows[base + patches : base + patches + 1, :] = message[i]
            rows[base + patches + 1 : base + tokens, :] = jnp.zeros(
                (tokens - patches - 1, width), f32
            )
        base, _ = norm_stats(rows[...])
        normed[...] = (
            base * nat[block + 4 : block + 5, :] + nat[block + 5 : block + 6, :]
        ).astype(bf16)
        total[...] = jnp.zeros_like(total)

    place_weight(weight, own, near, far, place, slot)
    projected = (nn(normed[...], weight[:, : 3 * local]) + bias_ref[...]).astype(bf16)
    qkv_out[...] = projected
    key_ok = lax.broadcasted_iota(jnp.int32, (tokens, tokens), 1) <= patches
    blank = jnp.zeros((tokens, width // 3 - local), bf16)
    for i in range(frames):
        part = projected[i * tokens : (i + 1) * tokens]
        pieces = [blank]
        for j in range(heads):
            q = part[:, j * HS : (j + 1) * HS]
            k = part[:, local + j * HS : local + (j + 1) * HS]
            v = part[:, 2 * local + j * HS : 2 * local + (j + 1) * HS]
            scores = jnp.where(key_ok, nt(q, k) * score_scale, masked_score)
            scores = jnp.exp(scores - jnp.max(scores, axis=-1, keepdims=True))
            probs = (scores * (1.0 / jnp.sum(scores, axis=-1, keepdims=True))).astype(bf16)
            probs_out[i * heads + j] = probs
            pieces.append(nn(probs, v).astype(bf16))
        context = jnp.concatenate(pieces, axis=1)
        ctx_out[pl.ds(i * tokens, tokens), :] = context
        total[pl.ds(i * tokens, tokens), :] += nt(context, weight[:, 2 * width // 3 :])

    @pl.when(slot == pl.num_programs(0) - 1)
    def _():
        s2_out[...] = rows[...] + total[...] + nat[block + 6 : block + 7, :]


def mlp_forward(
    scalars, s2_ref, nat, fc_bias_ref,
    fc_own, fc_near, fc_far, proj_own, proj_near, proj_far,
    pre_out, o0, o1, o2, o3, cls_out, normed, fc, proj, total, *, block, tokens,
):
    slot = pl.program_id(0)
    head_index, place = scalars[0], scalars[1]

    @pl.when(slot == 0)
    def _():
        base, _ = norm_stats(s2_ref[...])
        normed[...] = (
            base * nat[block + 7 : block + 8, :] + nat[block + 8 : block + 9, :]
        ).astype(bf16)
        total[...] = jnp.zeros_like(total)

    place_weight(fc, fc_own, fc_near, fc_far, place, slot)
    place_weight(proj, proj_own, proj_near, proj_far, place, slot)
    pre = nn(normed[...], fc[...]) + fc_bias_ref[...]
    pre_out[...] = pre
    hidden = (pre * jax.nn.sigmoid(gelu_rate * pre)).astype(bf16)
    total[...] += nn(hidden, proj[...])

    @pl.when(slot == pl.num_programs(0) - 1)
    def _():
        total[...] = s2_ref[...] + total[...] + nat[block + 9 : block + 10, :]
        frames, patches, _ = o0.shape
        cls = []
        for i in range(frames):
            base = i * tokens
            split_features(
                total[base : base + patches, :].astype(bf16), (o0, o1, o2, o3), i, head_index
            )
            cls.append(total[base : base + 1, :])
        cls_out[...] = put_rows(cls, head_index * frames, block)


def mlp_backward(
    scalars, u0, u1, u2, u3, cls_ref, s2_ref, pre_ref, nat,
    fc_own, fc_near, fc_far, proj_own, proj_near, proj_far,
    keep, send, fc_bias_out, vec_out, g2_out,
    normed, grad3, fc, proj, total, *, block, tokens,
):
    slot = pl.program_id(0)
    head_index, place = scalars[0], scalars[1]
    frames, patches, _ = u0.shape
    width = nat.shape[1]

    @pl.when(slot == 0)
    def _():
        base, _ = norm_stats(s2_ref[...])
        normed[...] = (
            base * nat[block + 7 : block + 8, :] + nat[block + 8 : block + 9, :]
        ).astype(bf16)
        lines = pick_rows(cls_ref[...], head_index * frames, frames)
        token = lax.broadcasted_iota(jnp.int32, (patches, 1), 0)
        for i in range(frames):
            base = i * tokens
            value = join_features((u0, u1, u2, u3), i, head_index).astype(f32)
            grad3[base : base + patches, :] = value + jnp.where(token == 0, lines[i], 0.0)
            grad3[base + patches : base + tokens, :] = jnp.zeros((tokens - patches, width), f32)
        total[...] = jnp.zeros_like(total)

    place_weight(fc, fc_own, fc_near, fc_far, place, slot)
    place_weight(proj, proj_own, proj_near, proj_far, place, slot)
    mlp_grad = grad3[...].astype(bf16)
    pre = pre_ref[...]
    gate = jax.nn.sigmoid(gelu_rate * pre)
    hidden = (pre * gate).astype(bf16)
    spread_grad(keep.at[1], send.at[1], tn(hidden, mlp_grad), place)
    hidden_grad = nt(mlp_grad, proj[...])
    pre_grad = (hidden_grad * (gate + gelu_rate * pre * gate * (1.0 - gate))).astype(bf16)
    fc_bias_out[...] = jnp.sum(pre_grad.astype(f32), axis=0, keepdims=True)
    spread_grad(keep.at[0], send.at[0], tn(normed[...], pre_grad), place)
    total[...] += nt(pre_grad, fc[...])

    @pl.when(slot == pl.num_programs(0) - 1)
    def _():
        base, factor = norm_stats(s2_ref[...])
        grad_in, gain_grad, shift_grad = norm_back(
            total[...], base, factor, nat[block + 7 : block + 8, :]
        )
        g2_out[...] = grad3[...] + grad_in
        vec_out[0:1, :] = gain_grad
        vec_out[1:2, :] = shift_grad
        vec_out[2:3, :] = jnp.sum(grad3[...].astype(bf16).astype(f32), axis=0, keepdims=True)
        vec_out[3:8, :] = jnp.zeros((5, width), f32)


def attention_backward(
    scalars, g2_ref, rows, qkv_ref, probs_ref, nat, mlp_vec, fc_bias_grad, own, near, far,
    dproj, v0, v1, v2, v3, o0, o1, o2, o3, msg_out,
    grad, sums, weight, total, *, heads, block, tokens,
):
    slot = pl.program_id(0)
    head_index, place = scalars[0], scalars[1]
    frames, patches, _ = o0.shape
    width = nat.shape[1]
    local = heads * HS
    wide = width // 3

    @pl.when(slot == 0)
    def _():
        grad[...] = g2_ref[...].astype(bf16)
        total[...] = jnp.zeros_like(total)

    place_weight(weight, own, near, far, place, slot)
    context_grad = nn(grad[...], weight[:, 2 * wide :]).astype(bf16)
    skip = wide - local
    for i in range(frames):
        span = slice(i * tokens, (i + 1) * tokens)
        dq, dk, dv = [], [], []
        for j in range(heads):
            q = qkv_ref[span, j * HS : (j + 1) * HS]
            k = qkv_ref[span, local + j * HS : local + (j + 1) * HS]
            v = qkv_ref[span, 2 * local + j * HS : 2 * local + (j + 1) * HS]
            cg = context_grad[span, skip + j * HS : skip + (j + 1) * HS]
            low = probs_ref[i * heads + j]
            probs = low.astype(f32)
            weighted = probs * nt(cg, v)
            score_grad = (
                weighted - probs * jnp.sum(weighted, axis=-1, keepdims=True)
            ).astype(bf16)
            dq.append((nn(score_grad, k) * score_scale).astype(bf16))
            dk.append((tn(score_grad, q) * score_scale).astype(bf16))
            dv.append(tn(low, cg).astype(bf16))
        dproj[pl.ds(i * tokens, tokens), :] = jnp.concatenate(
            dq + dk + dv + [jnp.zeros((tokens, width - 3 * local), bf16)], axis=1
        )
    all_grads = dproj[...]
    sums[pl.ds(slot, 1), :] = jnp.sum(all_grads.astype(f32), axis=0, keepdims=True)
    total[...] += nt(all_grads[:, : 3 * local], weight[:, : 3 * local])

    @pl.when(slot == pl.num_programs(0) - 1)
    def _():
        base, factor = norm_stats(rows[...])
        grad_in, gain_grad, shift_grad = norm_back(
            total[...], base, factor, nat[block + 4 : block + 5, :]
        )
        total[...] = grad_in + g2_ref[...]
        message = []
        for i in range(frames):
            first = i * tokens
            split_features(
                total[first : first + patches, :].astype(bf16), (o0, o1, o2, o3), i, head_index
            )
            message.append(total[first + patches : first + patches + 1, :])
        msg_out[...] = put_rows(message, head_index * frames, block)
        out_grad = jnp.sum(grad[...].astype(f32), axis=0, keepdims=True)
        for s, vec in enumerate((v0, v1, v2, v3)):
            vec[0:1, :] = gain_grad
            vec[1:2, :] = shift_grad
            vec[2:3, :] = out_grad
            vec[3:6, :] = mlp_vec[0:3, :]
            vec[6:7, :] = fc_bias_grad[s]
            vec[7:8, :] = sums[s : s + 1, :]


def attention_weights(scalars, g2_ref, normed, dproj, ctx, keep, send, grad):
    slot = pl.program_id(0)
    wide = normed.shape[1] // 3

    @pl.when(slot == 0)
    def _():
        grad[...] = g2_ref[...].astype(bf16)

    low_part = tn(normed[...], dproj[:, : 2 * wide])
    high_part = tn(normed[...], dproj[:, 2 * wide :]) + tn(grad[...], ctx[...])
    spread_grad(
        keep.at[0], send.at[0], jnp.concatenate([low_part, high_part], axis=1), scalars[1]
    )


def finish_mlp(scalars, near, far, fc_out, proj_out):
    here = (pl.program_id(0) ^ scalars[1]) % 2 == 0

    @pl.when(here)
    def _():
        fc_out[...] = near[0].astype(f32)
        proj_out[...] = near[1].astype(f32)

    @pl.when(jnp.logical_not(here))
    def _():
        fc_out[...] = far[0].astype(f32)
        proj_out[...] = far[1].astype(f32)


def finish_attention(scalars, near, far, qkv_out, out_out, rows):
    place = scalars[1]
    block = near.shape[2]
    for k in range(near.shape[0]):
        for c, piece in enumerate((near, far)):
            first = ((2 * k + c) ^ place) * block
            rows[pl.ds(pl.multiple_of(first, 32), block), :] = piece[k, 0].astype(f32)
    local = qkv_out.shape[2]
    for c in range(3):
        qkv_out[:, c, :] = rows[:, c * local : (c + 1) * local]
    out_out[...] = rows[:, 3 * local :].T


def finish_frames(scalars, p0, p1, p2, p3, add, out):
    frames = p0.shape[0]
    for s, piece in enumerate((p0, p1, p2, p3)):
        first = ((scalars[0] - s + 4) % 4) * frames
        for i in range(frames):
            out[first + i] = piece[i].astype(out.dtype)
    if add is not None:
        for i in range(out.shape[0]):
            out[i, 0:1, :] = out[i, 0:1, :] + add[i : i + 1, :]


def finish_output(scalars, p0, p1, p2, p3, out):
    finish_frames(scalars, p0, p1, p2, p3, None, out)

def whole(array):
    count = array.ndim
    return pl.BlockSpec(array.shape, lambda s, sc: (0,) * count)


def first_rows(array, rows):
    return pl.BlockSpec((rows, array.shape[1]), lambda s, sc: (0, 0))


def per_slot(array):
    count = array.ndim - 1
    return pl.BlockSpec((None,) + array.shape[1:], lambda s, sc: (s,) + (0,) * count)


def weight_specs(own, near, which):
    def pick(s, sc):
        return (0, 0, jnp.maximum(s - 1, 0), which, 0, 0)

    far_spec = pl.BlockSpec((2, 4, None, None) + near.shape[4:], pick)
    return [pl.BlockSpec(own.shape, lambda s, sc: (0, 0)), far_spec, far_spec]


def shaped(shape, dtype):
    return jax.ShapeDtypeStruct(tuple(shape), dtype)


def slot_out(shape, dtype, slots):
    count = len(shape)
    return (
        shaped((slots,) + tuple(shape), dtype),
        pl.BlockSpec((None,) + tuple(shape), lambda s, sc: (s,) + (0,) * count),
    )


def full_out(shape, dtype):
    count = len(shape)
    return shaped(shape, dtype), pl.BlockSpec(tuple(shape), lambda s, sc: (0,) * count)


def call(kernel, steps, scalars, inputs, outs, scratch=(), flops=0):
    inputs = [a if isinstance(a, tuple) else (a, whole(a)) for a in inputs]
    arrays, specs = zip(*inputs)
    shapes, out_specs = zip(*outs)
    moved = sum(a.size * a.dtype.itemsize for a in arrays + shapes)
    return pl.pallas_call(
        kernel,
        grid_spec=pltpu.PrefetchScalarGridSpec(
            num_scalar_prefetch=1,
            grid=(steps,),
            in_specs=list(specs),
            out_specs=list(out_specs),
            scratch_shapes=list(scratch),
        ),
        out_shape=list(shapes),
        cost_estimate=pl.CostEstimate(flops=flops, bytes_accessed=moved, transcendentals=0),
    )(scalars, *arrays)


def call_once(kernel, inputs, outs):
    moved = sum(a.size * a.dtype.itemsize for a in list(inputs) + list(outs))
    return pl.pallas_call(
        kernel,
        in_specs=[pl.BlockSpec(memory_space=pltpu.VMEM)] * len(inputs),
        out_specs=[pl.BlockSpec(memory_space=pltpu.VMEM)] * len(outs),
        out_shape=list(outs),
        cost_estimate=pl.CostEstimate(flops=0, bytes_accessed=moved, transcendentals=0),
    )(*inputs)


def tie(first, second):
    return lax.optimization_barrier((first, second))


def gather_rows(value):
    for bit in frame_bits(GROUP):
        value = jnp.concatenate([value, swap_frames(value, bit)], axis=0)
    value = jnp.concatenate([value, swap_frames(value, 1)], axis=0)
    return [value] + [swap_frames(value, bit) for bit in (2, 4, 6)]


def gathered_places(frame_index):
    count = lax.axis_size("frames")
    far = jnp.arange(count // GROUP) * GROUP
    near = jnp.arange(GROUP)
    return frame_index ^ (near.reshape(4, 2, 1) + far).reshape(-1)


def gather_weights(mine):
    half = mine.shape[1] // 2
    count = lax.axis_size("heads")
    got = [to_heads(mine, step) for step in range(1, count)]
    first = jnp.stack([g[:, :half] for g in got])
    second = jnp.stack([g[:, half:] for g in got])
    first = jnp.stack([first, swap_frames(first, 2)])
    second = jnp.stack([second, swap_frames(second, 4)])
    first_far = swap_frames(first, 4)
    second_far = swap_frames(second, 2)
    near = jnp.stack(
        [
            jnp.concatenate([first, first_far], axis=0),
            jnp.concatenate([second, second_far], axis=0),
        ]
    )
    return near, swap_frames(near, 1)


def reduce_first(keep, got):
    half = keep.shape[4] // 2

    def summed(x, y, low):
        rows = slice(0, half) if low else slice(half, 2 * half)
        index = (slice(None), slice(None), x, y, rows)
        return keep[index].astype(f32) + got[index].astype(f32)

    both = slice(None)
    first_got = swap_frames(summed(1, both, True).astype(bf16), 2)
    second_got = swap_frames(summed(both, 1, False).astype(bf16), 4)
    return summed, first_got, second_got


def reduce_second(summed, first_got, second_got):
    def next_first(y):
        return summed(0, y, True) + first_got[:, :, y].astype(f32)

    def next_second(x):
        return summed(x, 0, False) + second_got[:, :, x].astype(f32)

    first_last = swap_frames(next_first(1).astype(bf16), 4)
    second_last = swap_frames(next_second(1).astype(bf16), 2)
    return next_first(0), next_second(0), first_last, second_last


def reduce_last(first, second, first_last, second_last):
    first = first + first_last.astype(f32)
    second = second + second_last.astype(f32)
    total = jnp.concatenate([first, second], axis=2).astype(bf16)
    for bit in frame_bits(GROUP):
        total = (total.astype(f32) + swap_frames(total, bit).astype(f32)).astype(bf16)
    own = total[0].astype(f32)
    for step in range(1, total.shape[0]):
        own = own + to_heads(total[step], -step).astype(f32)
    return own.astype(bf16)


def regather(rows):
    half = rows.shape[1] // 2
    first, second = rows[:, :half], rows[:, half:]
    first = jnp.stack([first, swap_frames(first, 2)])
    second = jnp.stack([second, swap_frames(second, 4)])
    first = jnp.concatenate([first, swap_frames(first, 4)], axis=0)
    second = jnp.concatenate([second, swap_frames(second, 2)], axis=0)
    second = jnp.stack([second[0], second[2], second[1], second[3]])
    near = jnp.concatenate([first, second], axis=2)
    return near, swap_frames(near, 1)


def on_device(
    frames_in,
    upstream,
    video_of_frame,
    group_ids,
    msg_fc_weight,
    msg_fc_bias,
    msg_gain,
    msg_shift,
    msg_qkv_weight,
    msg_qv_bias,
    courier_result_kernel,
    msg_out_bias,
    ln1_gain,
    ln1_shift,
    qkv_weight,
    qv_bias,
    picture_result_kernel,
    out_bias,
    ln2_gain,
    ln2_shift,
    fc_weight,
    fc_bias,
    proj_weight,
    proj_bias,
):
    block, patches, local = frames_in.shape
    width = msg_qkv_weight.shape[0]
    slots = lax.axis_size("heads")
    own_frames = block // slots
    heads = local // HS
    tokens = -(-(patches + 1) // 16) * 16
    rows = own_frames * tokens
    hidden_local = fc_weight.shape[1]
    frame_index = lax.axis_index("frames")
    head_index = lax.axis_index("heads")
    place = frame_index % GROUP
    scalars = jnp.stack([head_index, place]).astype(jnp.int32)
    steps = range(1, slots)
    sizes = dict(block=block, tokens=tokens)

    def exchange(array):
        def frames_of(step):
            start = jnp.mod(head_index + step, slots) * own_frames
            return lax.dynamic_slice_in_dim(array, start, own_frames, axis=0)

        return [frames_of(0)] + [to_heads(frames_of(s), s) for s in steps]

    def to_all_heads(value):
        return [value] + [to_heads(value, s) for s in steps]

    def own_features(array):
        return lax.dynamic_slice_in_dim(array, head_index * local, local, axis=array.ndim - 1)

    def my_rows(array):
        size = array.shape[0] // GROUP
        return lax.dynamic_slice_in_dim(array, place * size, size, axis=0)

    cls_own = frames_in[:, 0, :]
    vectors = jnp.concatenate(
        [
            msg_fc_bias, msg_gain, msg_shift, msg_out_bias, ln1_gain, ln1_shift,
            out_bias, ln2_gain, ln2_shift, proj_bias,
        ]
    ).reshape(-1, local)
    lane = jnp.arange(width, dtype=jnp.int32)[None, :] // local
    vectors = jnp.where(lane == head_index, jnp.tile(vectors, (1, slots)), 0.0)
    qkv_bias = jnp.concatenate([qv_bias[0], jnp.zeros((local,), bf16), qv_bias[1], jnp.zeros((local,), bf16)])
    small = jnp.concatenate(
        [
            nn(cls_own, msg_fc_weight),
            vectors.astype(f32),
            fc_bias.reshape(1, -1).astype(f32),
            qkv_bias.reshape(1, -1).astype(f32),
            jnp.zeros((24 - block - 12, width), f32),
        ],
        axis=0,
    )
    small = to_all_heads(small)
    nat = sum(small)
    fc_bias_slots = jnp.stack([part[block + 10 : block + 11] for part in small])
    qkv_bias_slots = jnp.stack([part[block + 11 : block + 12, : 3 * local] for part in small])

    x_pieces = exchange(frames_in)

    attn_own = jnp.concatenate(
        [qkv_weight.reshape(width, 3 * local), picture_result_kernel.T], axis=1
    )
    attn_near, attn_far = gather_weights(my_rows(attn_own)[None])
    mlp_near, mlp_far = gather_weights(jnp.stack([my_rows(fc_weight), my_rows(proj_weight)]))
    attn_weights = list(
        zip((attn_own, attn_near, attn_far), weight_specs(attn_own, attn_near, 0))
    )
    mlp_weights = list(
        zip(
            (fc_weight, mlp_near, mlp_far, proj_weight, mlp_near, mlp_far),
            weight_specs(fc_weight, mlp_near, 0) + weight_specs(proj_weight, mlp_near, 1),
        )
    )

    sent = jnp.concatenate(
        [nat[:block], cls_own.astype(f32), jnp.zeros((block, 64), f32)], axis=1
    )
    start_pieces = gather_rows(sent)
    ids = video_of_frame.reshape(-1, block)[gathered_places(frame_index)].reshape(-1)
    ids_row, ids_col = ids[None, :], ids[:, None]
    total_frames = ids.shape[0]
    msg_bias = jnp.concatenate([msg_qv_bias[0], jnp.zeros((local,), bf16), msg_qv_bias[1]])
    start, cls_all, msg_rows, msg_proj, msg_probs, msg_context, msg_part = call_once(
        functools.partial(message_forward, heads=heads, block=block),
        start_pieces
        + [ids_col, ids_row, nat, msg_qkv_weight, msg_bias[None].astype(f32), courier_result_kernel],
        [
            shaped((total_frames, width), f32),
            shaped((total_frames, local), bf16),
            shaped((total_frames, width), bf16),
            shaped((total_frames, 3 * local), bf16),
            shaped((heads, total_frames, total_frames), f32),
            shaped((total_frames, local), bf16),
            shaped((block, width), f32),
        ],
    )
    msg_parts = to_all_heads(msg_part)

    wide = width // 3
    qkv, probs, context, stream_one, normed_one, stream_two = call(
        functools.partial(attention_forward, heads=heads, **sizes),
        slots,
        scalars,
        x_pieces
        + msg_parts
        + [(start, first_rows(start, block)), nat, (qkv_bias_slots, per_slot(qkv_bias_slots))]
        + attn_weights,
        [
            slot_out((rows, 3 * local), bf16, slots),
            slot_out((own_frames * heads, tokens, tokens), bf16, slots),
            slot_out((rows, wide), bf16, slots),
            full_out((rows, width), f32),
            full_out((rows, width), bf16),
            full_out((rows, width), f32),
        ],
        [pltpu.VMEM((width, width), bf16), pltpu.VMEM((rows, width), f32)],
        2 * rows * width * width * slots,
    )

    frame_out = shaped((own_frames, patches, local), bf16)
    pre, out_0, out_1, out_2, out_3, cls_block = call(
        functools.partial(mlp_forward, **sizes),
        slots,
        scalars,
        [stream_two, nat, (fc_bias_slots, per_slot(fc_bias_slots))] + mlp_weights,
        [slot_out((rows, hidden_local), f32, slots)]
        + [full_out(frame_out.shape, bf16)] * slots
        + [full_out((block, width), f32)],
        [
            pltpu.VMEM((rows, width), bf16),
            pltpu.VMEM((width, hidden_local), bf16),
            pltpu.VMEM((hidden_local, width), bf16),
            pltpu.VMEM((rows, width), f32),
        ],
        4 * rows * width * hidden_local * slots,
    )

    cls_pieces = gather_rows(sum(to_all_heads(cls_block)))
    videos = group_ids.shape[0]
    groups = jnp.pad(group_ids, (0, -videos % 8), constant_values=-1)
    loss_value, cls_grad = call_once(
        functools.partial(contrast, videos=videos, block=block),
        cls_pieces + [ids_row, ids_col, groups[:, None], groups[None, :]],
        [shaped((1, 1), f32), shaped((block, width), f32)],
    )

    up_pieces = exchange(upstream)
    out_pieces = [out_0] + [to_heads(o, s) for s, o in zip(steps, (out_1, out_2, out_3))]

    piece = (2, 2, width // GROUP, width)
    keep, send, fc_bias_grad, mlp_vec, grad_two = call(
        functools.partial(mlp_backward, **sizes),
        slots,
        scalars,
        up_pieces + [cls_grad, stream_two, (pre, per_slot(pre)), nat] + mlp_weights,
        [
            slot_out((2,) + piece, bf16, slots),
            slot_out((2,) + piece, bf16, slots),
            slot_out((1, hidden_local), f32, slots),
            full_out((8, width), f32),
            full_out((rows, width), f32),
        ],
        [
            pltpu.VMEM((rows, width), bf16),
            pltpu.VMEM((rows, width), f32),
            pltpu.VMEM((width, hidden_local), bf16),
            pltpu.VMEM((hidden_local, width), bf16),
            pltpu.VMEM((rows, width), f32),
        ],
        8 * rows * width * hidden_local * slots,
    )
    mlp_got = swap_frames(send, 1)

    dproj, vec_0, vec_1, vec_2, vec_3, gi_0, gi_1, gi_2, gi_3, grad_msg_block = call(
        functools.partial(attention_backward, heads=heads, **sizes),
        slots,
        scalars,
        [grad_two, stream_one, (qkv, per_slot(qkv)), (probs, per_slot(probs)), nat, mlp_vec, fc_bias_grad]
        + attn_weights,
        [slot_out((rows, width), bf16, slots)]
        + [full_out((8, width), f32)] * slots
        + [full_out(frame_out.shape, bf16)] * slots
        + [full_out((block, width), f32)],
        [
            pltpu.VMEM((rows, width), bf16),
            pltpu.VMEM((8, width), f32),
            pltpu.VMEM((width, width), bf16),
            pltpu.VMEM((rows, width), f32),
        ],
        6 * rows * width * width * slots,
    )
    dproj, mlp_got = tie(dproj, mlp_got)
    mlp_state = reduce_first(keep, mlp_got)
    attn_keep, attn_send = call(
        attention_weights,
        slots,
        scalars,
        [grad_two, normed_one, (dproj, per_slot(dproj)), (context, per_slot(context))],
        [slot_out((1,) + piece, bf16, slots), slot_out((1,) + piece, bf16, slots)],
        [pltpu.VMEM((rows, width), bf16)],
        2 * rows * width * width * slots,
    )
    attn_got = swap_frames(attn_send, 1)
    msg_heads = to_all_heads(grad_msg_block)
    msg_pieces = gather_rows(sum(msg_heads))

    (
        grad_message, grad_msg_qkv_weight, grad_msg_out_weight, back_own, back_send, msg_bias_sum, msg_sums,
    ) = call_once(
        functools.partial(message_back_one, heads=heads),
        msg_pieces + [msg_rows, msg_proj, msg_probs, msg_context, msg_qkv_weight, courier_result_kernel],
        [
            shaped((total_frames, width), f32),
            shaped((width, 3, local), f32),
            shaped((local, width), f32),
            shaped((total_frames, width), f32),
            shaped((total_frames, width), bf16),
            shaped((1, width), f32),
            shaped((3, local), f32),
        ],
    )
    back = [back_own] + [to_heads(back_send, s) for s in steps]
    attn_state = reduce_first(attn_keep, attn_got)
    mlp_state = reduce_second(*mlp_state)
    grad_msg_fc_weight, msg_vec, cls_back = call_once(
        functools.partial(message_back_two, block=block),
        back + [grad_message, start, cls_all, nat, msg_fc_weight],
        [shaped((local, width), f32), shaped((3, width), f32), shaped((block, local), f32)],
    )
    attn_state = reduce_second(*attn_state)
    grad_pieces = [gi_0] + [to_heads(g, s) for s, g in zip(steps, (gi_1, gi_2, gi_3))]

    mlp_near, mlp_far = regather(reduce_last(*mlp_state))
    attn_near, attn_far = regather(reduce_last(*attn_state))

    vec = vec_0 + sum(to_heads(v, -s) for s, v in zip(steps, (vec_1, vec_2, vec_3)))
    for bit in frame_bits():
        vec = vec + swap_frames(vec, bit)

    def picked(s, sc):
        return ((s ^ sc[1]) // 2, 0, 0, 0)

    part_spec = pl.BlockSpec((None,) + mlp_near.shape[1:], picked)
    out_spec = pl.BlockSpec((width // GROUP, width), lambda s, sc: (s, 0))
    grad_fc_weight, grad_proj_weight = call(
        finish_mlp,
        GROUP,
        scalars,
        [(mlp_near, part_spec), (mlp_far, part_spec)],
        [(shaped((width, width), f32), out_spec)] * 2,
    )
    grad_qkv_weight, grad_out_weight = call(
        finish_attention,
        1,
        scalars,
        [attn_near, attn_far],
        [full_out((width, 3, local), f32), full_out((local, width), f32)],
        [pltpu.VMEM((width, width), f32)],
    )
    (output,) = call(
        finish_output, 1, scalars, out_pieces, [full_out((block, patches, local), bf16)]
    )
    (grad_input,) = call(
        finish_frames, 1, scalars, grad_pieces + [cls_back], [full_out((block, patches, local), f32)]
    )
    own = own_features(jnp.concatenate([vec[:6], msg_vec, msg_bias_sum], axis=0))
    return (
        output,
        loss_value.reshape(()),
        grad_input,
        grad_msg_fc_weight,
        own[8],
        own[6],
        own[7],
        grad_msg_qkv_weight,
        jnp.stack([msg_sums[0], msg_sums[2]]),
        grad_msg_out_weight,
        own[9],
        own[0],
        own[1],
        grad_qkv_weight,
        jnp.stack([vec[7, :local], vec[7, 2 * local : 3 * local]]),
        grad_out_weight,
        own[2],
        own[3],
        own[4],
        grad_fc_weight,
        vec[6],
        grad_proj_weight,
        own[5],
    )


def solution(mesh):
    placed = (
        P("frames", None, "heads"),
        P("frames", None, "heads"),
        P(),
        P(),
        P("heads", None),
        P("heads"),
        P("heads"),
        P("heads"),
        P(None, None, "heads"),
        P(None, "heads"),
        P("heads", None),
        P("heads"),
        P("heads"),
        P("heads"),
        P(None, None, "heads"),
        P(None, "heads"),
        P("heads", None),
        P("heads"),
        P("heads"),
        P("heads"),
        P(None, "heads"),
        P("heads"),
        P("heads", None),
        P("heads"),
    )
    return jax.shard_map(
        on_device,
        mesh=mesh,
        in_specs=placed,
        out_specs=(
            P("frames", None, "heads"),
            P(),
            P("frames", None, "heads"),
            P("heads", None),
            P("heads"),
            P("heads"),
            P("heads"),
            P(None, None, "heads"),
            P(None, "heads"),
            P("heads", None),
            P("heads"),
            P("heads"),
            P("heads"),
            P(None, None, "heads"),
            P(None, "heads"),
            P("heads", None),
            P("heads"),
            P("heads"),
            P("heads"),
            P(None, "heads"),
            P("heads"),
            P("heads", None),
            P("heads"),
        ),
        check_vma=False,
    )
```

```python
import functools

import jax
import jax.numpy as jnp
from jax import lax
from jax.experimental import pallas as pl
from jax.experimental.pallas import tpu as pltpu
from jax.sharding import PartitionSpec as P

HS = 64
GROUP = 8

norm_eps = 1e-05
score_scale = 0.125
gelu_rate = 1.702
contrast_sharpness = 0.02
masked_score = -1000000000.0
exact = lax.Precision.HIGHEST
f32 = jnp.float32
bf16 = jnp.bfloat16

PIECES = ((0, 2, 4, 6), (0, 4, 2, 6))


def nn(left, right):
    return lax.dot_general(left, right, (((1,), (0,)), ((), ())), preferred_element_type=f32)


def nt(left, right):
    return lax.dot_general(left, right, (((1,), (1,)), ((), ())), preferred_element_type=f32)


def tn(left, right):
    return lax.dot_general(left, right, (((0,), (0,)), ((), ())), preferred_element_type=f32)


def to_heads(value, step):
    count = lax.axis_size("heads")
    return lax.ppermute(value, "heads", [(i, (i + step) % count) for i in range(count)])


def swap_frames(value, bit):
    count = lax.axis_size("frames")
    return lax.ppermute(value, "frames", [(i, i ^ bit) for i in range(count)])


def frame_bits(start=1):
    count = lax.axis_size("frames")
    bits = []
    bit = start
    while bit < count:
        bits.append(bit)
        bit *= 2
    return bits


def norm_stats(rows):
    center = jnp.mean(rows, axis=-1, keepdims=True)
    offset = rows - center
    factor = lax.rsqrt(jnp.mean(offset * offset, axis=-1, keepdims=True) + norm_eps)
    return offset * factor, factor


def norm_back(grad_out, normed, factor, gain):
    scaled = grad_out * gain
    first = jnp.mean(scaled, axis=-1, keepdims=True)
    second = jnp.mean(scaled * normed, axis=-1, keepdims=True)
    grad_in = factor * (scaled - first - normed * second)
    return (
        grad_in,
        jnp.sum(grad_out * normed, axis=0, keepdims=True),
        jnp.sum(grad_out, axis=0, keepdims=True),
    )


def place_weight(target, own, near, far, place, slot):
    block = target.shape[0] // GROUP
    half = block // 2

    @pl.when(slot == 0)
    def _():
        target[...] = own[...]

    @pl.when(slot > 0)
    def _():
        for q in range(2):
            for j in range(4):
                here = (place ^ PIECES[q][j]) * block + q * half
                there = (place ^ PIECES[q][j] ^ 1) * block + q * half
                target[pl.ds(pl.multiple_of(here, 16), half), :] = near[q, j]
                target[pl.ds(pl.multiple_of(there, 16), half), :] = far[q, j]


def pick_rows(array, first, count):
    row = lax.broadcasted_iota(jnp.int32, (array.shape[0], 1), 0)
    return [
        jnp.sum(jnp.where(row == first + i, array, 0.0), axis=0, keepdims=True)
        for i in range(count)
    ]


def put_rows(rows, first, total):
    row = lax.broadcasted_iota(jnp.int32, (total, 1), 0)
    value = jnp.zeros((total, rows[0].shape[1]), f32)
    for i, line in enumerate(rows):
        value = jnp.where(row == first + i, line, value)
    return value


def contrast(
    p0, p1, p2, p3, ids_row, ids_col, group_col, group_row, loss_out, grad_out, *, videos, block
):
    each = p0.shape[0]
    padded = group_col.shape[0]
    video = lax.broadcasted_iota(jnp.int32, (padded, 1), 0)
    onehot = (ids_row[...] == video).astype(f32)
    counts = jnp.sum(onehot, axis=1, keepdims=True)
    counts = jnp.where(video < videos, counts, 1.0)
    pooled = None
    for j, piece in enumerate((p0, p1, p2, p3)):
        hot = (ids_row[:, j * each : (j + 1) * each] == video).astype(f32)
        term = jnp.dot(hot, piece[...], precision=exact, preferred_element_type=f32)
        pooled = term if pooled is None else pooled + term
    pooled = pooled / counts
    scale = lax.rsqrt(jnp.sum(pooled * pooled, axis=1, keepdims=True) + 1e-06)
    unit = pooled * scale
    logits = (
        lax.dot_general(
            unit, unit, (((1,), (1,)), ((), ())), precision=exact, preferred_element_type=f32
        )
        / contrast_sharpness
    )
    other = lax.broadcasted_iota(jnp.int32, (padded, padded), 1)
    this = lax.broadcasted_iota(jnp.int32, (padded, padded), 0)
    usable = jnp.logical_and(other != this, other < videos)
    logits = jnp.where(usable, logits, masked_score)
    top = jnp.max(logits, axis=1, keepdims=True)
    powers = jnp.exp(logits - top)
    total = jnp.sum(powers, axis=1, keepdims=True)
    log_total = top + jnp.log(total)
    real = jnp.logical_and(usable, this < videos)
    positive = jnp.where(
        jnp.logical_and(group_col[...] == group_row[...], real), 1.0, 0.0
    )
    weights = positive / jnp.maximum(jnp.sum(positive, axis=1, keepdims=True), 1.0)
    each_loss = jnp.where(real, weights * (log_total - logits), 0.0)
    loss_out[...] = jnp.sum(jnp.sum(each_loss, axis=1, keepdims=True), axis=0, keepdims=True)
    g_logits = jnp.sum(weights, axis=1, keepdims=True) * (powers / total) - weights
    g_logits = jnp.where(real, g_logits, 0.0)
    g_unit = jnp.dot(g_logits, unit, precision=exact, preferred_element_type=f32)
    g_unit = g_unit + lax.dot_general(
        g_logits, unit, (((0,), (0,)), ((), ())), precision=exact, preferred_element_type=f32
    )
    g_unit = g_unit / contrast_sharpness
    inner = jnp.sum(pooled * g_unit, axis=1, keepdims=True)
    g_pooled = scale * g_unit - scale * scale * scale * inner * pooled
    hot = (ids_col[:block, :] == lax.broadcasted_iota(jnp.int32, (block, padded), 1)).astype(f32)
    grad_out[...] = jnp.dot(hot, g_pooled / counts, precision=exact, preferred_element_type=f32)


def spread_grad(keep, send, matrix, slot_value, place):
    block = slot_value.shape[0] // GROUP
    for owner in range(GROUP):
        part = slot_value[owner * block : (owner + 1) * block].astype(bf16)
        offset = place ^ owner
        rest = offset // 2
        mine = offset % 2 == 0

        @pl.when(mine)
        def _():
            keep[rest % 2, rest // 2, matrix, 0:block, :] = part

        @pl.when(jnp.logical_not(mine))
        def _():
            send[rest % 2, rest // 2, matrix, 0:block, :] = part


def join_features(pieces, own, i, head_index, turned, tokens):
    local, patches = own.shape[1:]
    count = turned.shape[0] // local
    for s in range(count):
        block = (head_index - s + count) % count
        value = own[i] if s == 0 else pieces(s, i)
        turned[pl.ds(pl.multiple_of(block * local, 64), local), 0:patches] = value
    token = lax.broadcasted_iota(jnp.int32, (tokens, 1), 0)
    return jnp.where(token < patches, turned[...].T[:tokens], 0)


def split_features(value, pieces, i, head_index, turned):
    local, patches = pieces[0].shape[1:]
    turned[:, 0 : value.shape[0]] = value.T
    for s, piece in enumerate(pieces):
        block = (head_index + s) % len(pieces)
        piece[i] = turned[pl.ds(pl.multiple_of(block * local, 64), local), 0:patches]


SMALL = 32


def pack_first(
    scalars, x, fc, qkv, out, b0, b1, b2, b3, b4, b5, b6, b7, b8, b9, qv, fcb,
    weight, cls, s1, s2, s3,
):
    head_index, place = scalars[0], scalars[1]
    block, local, patches = x.shape
    width = fc.shape[1]
    slots = width // local
    rows = width // GROUP
    for c in range(3):
        weight[c * local : (c + 1) * local, :] = qkv[c]
    weight[3 * local :, :] = out[...]
    lane = lax.broadcasted_iota(jnp.int32, (1, width), 1) // local
    zero = jnp.zeros((1, local), f32)
    starts = []
    for f in range(block):
        part = x[f, :, 0:128]
        starts.append(tn(part, fc[...])[0:1])
        cls[f : f + 1, :] = part.T[0:1].astype(f32)
    start = jnp.concatenate(starts, axis=0)
    high = start.astype(bf16).astype(f32)
    lines = [high, start - high]
    for vec in (b0, b1, b2, b3, b4, b5, b6, b7, b8, b9):
        value = vec[...].reshape(1, local).astype(f32)
        lines.append(jnp.where(lane == head_index, jnp.concatenate([value] * slots, axis=1), 0.0))
    lines.append(fcb[...].reshape(1, width).astype(f32))
    lines.append(
        jnp.concatenate([qv[0:1, :].astype(f32), zero, qv[1:2, :].astype(f32), zero], axis=1)
    )
    lines.append(jnp.zeros((SMALL - 2 * block - 12, width), f32))
    small = jnp.concatenate(lines, axis=0).astype(bf16)
    mine = weight[pl.ds(pl.multiple_of(place * rows, 32), rows), :]
    third = 2 * local // 3
    for step, send in enumerate((s1, s2, s3)):
        send[0:SMALL, :] = small
        send[SMALL : SMALL + rows, :] = mine
        first = ((head_index + step + 1) % slots) * 2
        base = SMALL + rows
        rest = local - third
        send[base : base + third, 0:patches] = x[first, 0:third, :]
        send[base : base + rest, 256 : 256 + patches] = x[first, third:local, :]
        send[base + rest : base + third, 256 : 256 + patches] = x[first + 1, 0 : third - rest, :]
        send[base : base + third, 512 : 512 + patches] = x[first + 1, third - rest : local, :]


def unpack_first(
    scalars, x, cls, own, r1, r2, r3,
    nat, fc_bias, qkv_bias, sent, first_half, second_half, stream, turned, *, block, tokens,
):
    head_index = scalars[0]
    frames, local, patches = x.shape
    width = own.shape[1]
    rows = width // GROUP
    received = (own, r1, r2, r3)
    start = None
    vectors = None
    for s, piece in enumerate(received):
        small = piece[0:SMALL, :].astype(f32)
        value = small[0:block] + small[block : 2 * block]
        vec = small[2 * block : 2 * block + 10]
        start = value if start is None else start + value
        vectors = vec if vectors is None else vectors + vec
        fc_bias[s] = small[2 * block + 10 : 2 * block + 11]
        qkv_bias[s] = small[2 * block + 11 : 2 * block + 12, : 3 * local]
    nat[0:10, :] = vectors
    nat[10:16, :] = jnp.zeros((6, width), f32)
    sent[:, 0:width] = start + vectors[0:1]
    sent[:, width : width + local] = cls[...]
    sent[:, width + local :] = jnp.zeros((block, sent.shape[1] - width - local), f32)
    for s in range(1, len(received)):
        piece = received[s]
        first_half[s - 1, 0] = piece[SMALL : SMALL + rows // 2, :]
        second_half[s - 1, 0] = piece[SMALL + rows // 2 : SMALL + rows, :]
    base = SMALL + rows
    third = 2 * local // 3
    rest = local - third

    def pieces(s, i):
        piece = received[s]
        if i == 0:
            low = piece[base : base + third, 0:patches]
            high = piece[base : base + rest, 256 : 256 + patches]
        else:
            low = piece[base + rest : base + third, 256 : 256 + patches]
            high = piece[base : base + third, 512 : 512 + patches]
        return jnp.concatenate([low, high], axis=0)

    for i in range(frames):
        stream[i * tokens : (i + 1) * tokens, :] = join_features(
            pieces, x, i, head_index, turned, tokens
        )


def message_forward(
    p0, p1, p2, p3, ids_col, ids_row, nat, weight, qv, courier,
    start_out, cls_out, rows_out, proj_out, probs_out, ctx_out, part_out, *, heads, block,
):
    width = nat.shape[1]
    local = heads * HS
    each = p0.shape[0]
    for j, piece in enumerate((p0, p1, p2, p3)):
        span = pl.ds(j * each, each)
        start_out[span, :] = piece[:, :width]
        cls_out[span, :] = piece[:, width : width + local].astype(bf16)
    base, _ = norm_stats(start_out[...])
    rows = (base * nat[1:2, :] + nat[2:3, :]).astype(bf16)
    rows_out[...] = rows
    bias = (qv[0:1, :].astype(f32), jnp.zeros((1, local), f32), qv[1:2, :].astype(f32))
    proj = [(nt(rows, weight[c]) + bias[c]).astype(bf16) for c in range(3)]
    proj_out[...] = jnp.concatenate(proj, axis=1)
    same = ids_col[...] == ids_row[...]
    context = []
    for j in range(heads):
        q, k, v = [p[:, j * HS : (j + 1) * HS] for p in proj]
        scores = jnp.where(same, nt(q, k) * score_scale, masked_score)
        scores = jnp.exp(scores - jnp.max(scores, axis=-1, keepdims=True))
        probs = scores / jnp.sum(scores, axis=-1, keepdims=True)
        probs_out[j] = probs
        context.append(nn(probs.astype(bf16), v).astype(bf16))
    context = jnp.concatenate(context, axis=1)
    ctx_out[...] = context
    part_out[...] = nn(context[:16], courier[...])[:block]


def message_back_one(
    scalars, p0, p1, p2, p3, rows, proj, probs_ref, ctx, weight, courier,
    grad_out, weight_out, courier_out, back_out, send_out, bias_out, qv_out, *, heads,
):
    local = heads * HS
    each = p0.shape[0]
    for j, piece in enumerate((p0, p1, p2, p3)):
        grad_out[pl.ds(j * each, each), :] = piece[...]
    grad = grad_out[...].astype(bf16)
    bias_out[...] = own_part(
        jnp.sum(grad.astype(f32), axis=0, keepdims=True), local, scalars[0]
    ).reshape(local)
    courier_out[...] = tn(ctx[...], grad)
    context_grad = nt(grad, courier[...]).astype(bf16)
    dq, dk, dv = [], [], []
    for j in range(heads):
        q, k, v = [
            proj[:, c * local + j * HS : c * local + (j + 1) * HS] for c in range(3)
        ]
        cg = context_grad[:, j * HS : (j + 1) * HS]
        probs = probs_ref[j]
        weighted = probs * nt(cg, v)
        score_grad = (weighted - probs * jnp.sum(weighted, axis=-1, keepdims=True)).astype(bf16)
        dq.append((nn(score_grad, k) * score_scale).astype(bf16))
        dk.append((tn(score_grad, q) * score_scale).astype(bf16))
        dv.append(tn(probs.astype(bf16), cg).astype(bf16))
    back = None
    for c, parts in enumerate((dq, dk, dv)):
        value = jnp.concatenate(parts, axis=1)
        weight_out[c] = tn(value, rows[...])
        if c != 1:
            qv_out[c // 2 : c // 2 + 1, :] = jnp.sum(value.astype(f32), axis=0, keepdims=True)
        term = nn(value, weight[c])
        back = term if back is None else back + term
    back_out[...] = back
    send_out[...] = back.astype(bf16)


def own_part(line, local, head_index):
    part = line[:, 0:local]
    for b in range(1, line.shape[1] // local):
        part = jnp.where(head_index == b, line[:, b * local : (b + 1) * local], part)
    return part


def message_back_two(
    scalars, own, r1, r2, r3, grad, start, cls, nat, weight,
    weight_out, gain_out, shift_out, bias_out, cls_back_out,
):
    total = own[...]
    for piece in (r1, r2, r3):
        total = total + piece[...].astype(f32)
    base, factor = norm_stats(start[...])
    grad_in, gain_grad, shift_grad = norm_back(total, base, factor, nat[1:2, :])
    start_grad = (grad[...] + grad_in).astype(bf16)
    weight_out[...] = tn(cls[...], start_grad)
    local = weight.shape[0]
    lines = (gain_grad, shift_grad, jnp.sum(start_grad.astype(f32), axis=0, keepdims=True))
    for out, line in zip((gain_out, shift_out, bias_out), lines):
        out[...] = own_part(line, local, scalars[0]).reshape(local)
    cls_back_out[...] = nt(weight[...], start_grad[:16])


def attention_forward(
    scalars, stream, m0, m1, m2, m3, start, nat, bias_ref, own, near, far,
    qkv_out, probs_out, ctx_out, rows, normed, s2_out, weight, total, *, heads, tokens, patches,
):
    slot = pl.program_id(0)
    head_index, place = scalars[0], scalars[1]
    frames = stream.shape[0] // tokens
    local = heads * HS

    @pl.when(slot == 0)
    def _():
        lines = start[...] + m0[...] + m1[...] + m2[...] + m3[...] + nat[3:4, :]
        message = pick_rows(lines, head_index * frames, frames)
        token = lax.broadcasted_iota(jnp.int32, (tokens, 1), 0)
        for i in range(frames):
            span = slice(i * tokens, (i + 1) * tokens)
            rows[span, :] = jnp.where(token == patches, message[i], stream[span, :].astype(f32))
        base, _ = norm_stats(rows[...])
        normed[...] = (base * nat[4:5, :] + nat[5:6, :]).astype(bf16)
        total[...] = jnp.zeros_like(total)

    place_weight(weight, own, near, far, place, slot)
    projected = (nt(normed[...], weight[: 3 * local, :]) + bias_ref[...]).astype(bf16)
    qkv_out[...] = projected
    key_ok = lax.broadcasted_iota(jnp.int32, (tokens, tokens), 1) <= patches
    for i in range(frames):
        part = projected[i * tokens : (i + 1) * tokens]
        pieces = []
        for j in range(heads):
            q = part[:, j * HS : (j + 1) * HS]
            k = part[:, local + j * HS : local + (j + 1) * HS]
            v = part[:, 2 * local + j * HS : 2 * local + (j + 1) * HS]
            scores = jnp.where(key_ok, nt(q, k) * score_scale, masked_score)
            scores = jnp.exp(scores - jnp.max(scores, axis=-1, keepdims=True))
            probs = (scores * (1.0 / jnp.sum(scores, axis=-1, keepdims=True))).astype(bf16)
            probs_out[i * heads + j] = probs
            pieces.append(nn(probs, v).astype(bf16))
        ctx_out[pl.ds(i * tokens, tokens), :] = jnp.concatenate(pieces, axis=1)
    total[...] += nn(ctx_out[...], weight[3 * local :, :])

    @pl.when(slot == pl.num_programs(0) - 1)
    def _():
        s2_out[...] = rows[...] + total[...] + nat[6:7, :]


def mlp_forward(
    scalars, s2_ref, nat, fc_bias_ref,
    fc_own, fc_near, fc_far, proj_own, proj_near, proj_far,
    pre_out, o0, o1, o2, o3, cls_out, normed, fc, proj, total, turned, *, block, tokens,
):
    slot = pl.program_id(0)
    head_index, place = scalars[0], scalars[1]

    @pl.when(slot == 0)
    def _():
        base, _ = norm_stats(s2_ref[...])
        normed[...] = (base * nat[7:8, :] + nat[8:9, :]).astype(bf16)
        total[...] = jnp.zeros_like(total)

    place_weight(fc, fc_own, fc_near, fc_far, place, slot)
    place_weight(proj, proj_own, proj_near, proj_far, place, slot)
    pre = nn(normed[...], fc[...]) + fc_bias_ref[...]
    pre_out[...] = pre
    hidden = (pre * jax.nn.sigmoid(gelu_rate * pre)).astype(bf16)
    total[...] += nn(hidden, proj[...])

    @pl.when(slot == pl.num_programs(0) - 1)
    def _():
        total[...] = s2_ref[...] + total[...] + nat[9:10, :]
        frames = o0.shape[0]
        cls = []
        for i in range(frames):
            base = i * tokens
            split_features(
                total[base : base + tokens, :].astype(bf16), (o0, o1, o2, o3), i, head_index, turned
            )
            cls.append(total[base : base + 1, :])
        cls_out[...] = put_rows(cls, head_index * frames, block)


def mlp_backward(
    scalars, u0, u1, u2, u3, cls_ref, s2_ref, pre_ref, nat,
    fc_own, fc_near, fc_far, proj_own, proj_near, proj_far,
    keep, send, fc_bias_out, vec_out, g2_out,
    normed, grad3, fc, proj, total, turned, *, tokens,
):
    slot = pl.program_id(0)
    head_index, place = scalars[0], scalars[1]
    frames = u0.shape[0]
    width = nat.shape[1]

    @pl.when(slot == 0)
    def _():
        base, _ = norm_stats(s2_ref[...])
        normed[...] = (base * nat[7:8, :] + nat[8:9, :]).astype(bf16)
        lines = pick_rows(cls_ref[...], head_index * frames, frames)
        token = lax.broadcasted_iota(jnp.int32, (tokens, 1), 0)
        others = (u0, u1, u2, u3)
        for i in range(frames):
            value = join_features(
                lambda s, i: others[s][i], u0, i, head_index, turned, tokens
            ).astype(f32)
            grad3[i * tokens : (i + 1) * tokens, :] = value + jnp.where(token == 0, lines[i], 0.0)
        total[...] = jnp.zeros_like(total)

    place_weight(fc, fc_own, fc_near, fc_far, place, slot)
    place_weight(proj, proj_own, proj_near, proj_far, place, slot)
    mlp_grad = grad3[...].astype(bf16)
    pre = pre_ref[...]
    gate = jax.nn.sigmoid(gelu_rate * pre)
    hidden = (pre * gate).astype(bf16)
    spread_grad(keep, send, 1, tn(hidden, mlp_grad), place)
    hidden_grad = nt(mlp_grad, proj[...])
    pre_grad = (hidden_grad * (gate + gelu_rate * pre * gate * (1.0 - gate))).astype(bf16)
    fc_bias_out[...] = jnp.sum(pre_grad.astype(f32), axis=0, keepdims=True)
    spread_grad(keep, send, 0, tn(normed[...], pre_grad), place)
    total[...] += nt(pre_grad, fc[...])

    @pl.when(slot == pl.num_programs(0) - 1)
    def _():
        base, factor = norm_stats(s2_ref[...])
        grad_in, gain_grad, shift_grad = norm_back(total[...], base, factor, nat[7:8, :])
        g2_out[...] = grad3[...] + grad_in
        vec_out[0:1, :] = gain_grad
        vec_out[1:2, :] = shift_grad
        vec_out[2:3, :] = jnp.sum(grad3[...].astype(bf16).astype(f32), axis=0, keepdims=True)
        vec_out[3:8, :] = jnp.zeros((5, width), f32)


def attention_backward(
    scalars, g2_ref, rows, qkv_ref, probs_ref, nat, mlp_vec, fc_bias_grad, own, near, far,
    dproj, vec_out, o0, o1, o2, o3, msg_out,
    grad, sums, weight, total, turned, *, heads, block, tokens,
):
    slot = pl.program_id(0)
    head_index, place = scalars[0], scalars[1]
    frames, _, patches = o0.shape
    width = nat.shape[1]
    local = heads * HS

    @pl.when(slot == 0)
    def _():
        grad[...] = g2_ref[...].astype(bf16)
        total[...] = jnp.zeros_like(total)
        sums[...] = jnp.zeros_like(sums)

    place_weight(weight, own, near, far, place, slot)
    context_grad = nt(grad[...], weight[3 * local :, :]).astype(bf16)
    for i in range(frames):
        span = slice(i * tokens, (i + 1) * tokens)
        dq, dk, dv = [], [], []
        for j in range(heads):
            q = qkv_ref[span, j * HS : (j + 1) * HS]
            k = qkv_ref[span, local + j * HS : local + (j + 1) * HS]
            v = qkv_ref[span, 2 * local + j * HS : 2 * local + (j + 1) * HS]
            cg = context_grad[span, j * HS : (j + 1) * HS]
            low = probs_ref[i * heads + j]
            probs = low.astype(f32)
            weighted = probs * nt(cg, v)
            score_grad = (
                weighted - probs * jnp.sum(weighted, axis=-1, keepdims=True)
            ).astype(bf16)
            dq.append((nn(score_grad, k) * score_scale).astype(bf16))
            dk.append((tn(score_grad, q) * score_scale).astype(bf16))
            dv.append(tn(low, cg).astype(bf16))
        dproj[pl.ds(i * tokens, tokens), :] = jnp.concatenate(dq + dk + dv, axis=1)
    all_grads = dproj[...]
    sums[pl.ds(slot, 1), 0 : 3 * local] = jnp.sum(all_grads.astype(f32), axis=0, keepdims=True)
    total[...] += nn(all_grads, weight[: 3 * local, :])

    @pl.when(slot == pl.num_programs(0) - 1)
    def _():
        base, factor = norm_stats(rows[...])
        grad_in, gain_grad, shift_grad = norm_back(total[...], base, factor, nat[4:5, :])
        total[...] = grad_in + g2_ref[...]
        message = []
        for i in range(frames):
            first = i * tokens
            split_features(
                total[first : first + tokens, :].astype(bf16), (o0, o1, o2, o3), i, head_index, turned
            )
            message.append(total[first + patches : first + patches + 1, :])
        msg_out[...] = put_rows(message, head_index * frames, block)
        out_grad = jnp.sum(grad[...].astype(f32), axis=0, keepdims=True)
        for s in range(vec_out.shape[0]):
            vec_out[s, 0:1, :] = gain_grad
            vec_out[s, 1:2, :] = shift_grad
            vec_out[s, 2:3, :] = out_grad
            vec_out[s, 3:6, :] = mlp_vec[0:3, :]
            vec_out[s, 6:7, :] = fc_bias_grad[s]
            vec_out[s, 7:8, :] = sums[s : s + 1, :]


def attention_weights(scalars, g2_ref, normed, dproj, ctx, vec, keep, send, grad):
    slot = pl.program_id(0)
    place = scalars[1]

    @pl.when(slot == 0)
    def _():
        grad[...] = g2_ref[...].astype(bf16)

    value = jnp.concatenate([tn(dproj[...], normed[...]), tn(ctx[...], grad[...])], axis=0)
    spread_grad(keep, send, 0, value, place)
    block, width = value.shape[0] // GROUP, value.shape[1]
    blank = jnp.zeros((keep.shape[3] - block - 1, width), f32)
    for owner in range(GROUP):
        offset = place ^ owner
        rest = offset // 2
        tail = jnp.concatenate([vec[owner : owner + 1, :], blank], axis=0).astype(bf16)

        @pl.when(offset % 2 == 0)
        def _():
            keep[rest % 2, rest // 2, 0, block:, :] = tail

        @pl.when(offset % 2 == 1)
        def _():
            send[rest % 2, rest // 2, 0, block:, :] = tail


def finish_weights(scalars, near, far, fc_out, proj_out, qkv_out, out_out, vec_out, *, block):
    step = pl.program_id(0)
    here = (step ^ scalars[1]) % 2 == 0
    value = jnp.where(here, near[...], far[...]).astype(f32)
    fc_out[...] = value[0:block]
    proj_out[...] = value[block : 2 * block]
    vec_out[pl.ds(step, 1), :] = value[3 * block : 3 * block + 1]

    @pl.when(step < 6)
    def _():
        qkv_out[...] = value[2 * block : 3 * block]

    @pl.when(step >= 6)
    def _():
        out_out[...] = value[2 * block : 3 * block]


def finish_vectors(scalars, vec, o0, o1, o2, o3, o4, o5, fc_out, qv_out):
    local = o0.shape[0]
    for i, out in enumerate((o0, o1, o2, o3, o4, o5)):
        out[...] = own_part(vec[i : i + 1, :], local, scalars[0]).reshape(local)
    fc_out[...] = vec[6:7, :].reshape(vec.shape[1])
    qv_out[0:1, :] = vec[7:8, 0:local]
    qv_out[1:2, :] = vec[7:8, 2 * local : 3 * local]


def finish_output(scalars, p0, p1, p2, p3, out):
    frames = p0.shape[0]
    for s, piece in enumerate((p0, p1, p2, p3)):
        first = ((scalars[0] - s + 4) % 4) * frames
        for i in range(frames):
            out[first + i] = piece[i]


def finish_grads(scalars, p0, p1, p2, p3, add, out):
    frames, local, patches = p0.shape
    for s, piece in enumerate((p0, p1, p2, p3)):
        first = ((scalars[0] - s + 4) % 4) * frames
        for i in range(frames):
            out[first + i] = piece[i].astype(f32)
    lane = lax.broadcasted_iota(jnp.int32, (local, 128), 1)
    for f in range(out.shape[0]):
        out[f, :, 0:128] = out[f, :, 0:128] + jnp.where(lane == 0, add[:, f : f + 1], 0.0)


def whole(array):
    count = array.ndim
    return pl.BlockSpec(array.shape, lambda s, sc: (0,) * count)


def first_rows(array, rows):
    return pl.BlockSpec((rows, array.shape[1]), lambda s, sc: (0, 0))


def per_slot(array):
    count = array.ndim - 1
    return pl.BlockSpec((None,) + array.shape[1:], lambda s, sc: (s,) + (0,) * count)


def weight_specs(own, near, which):
    def pick(s, sc):
        return (0, 0, jnp.maximum(s - 1, 0), which, 0, 0)

    far_spec = pl.BlockSpec((2, 4, None, None) + near.shape[4:], pick)
    return [pl.BlockSpec(own.shape, lambda s, sc: (0, 0)), far_spec, far_spec]


def shaped(shape, dtype):
    return jax.ShapeDtypeStruct(tuple(shape), dtype)


def slot_out(shape, dtype, slots):
    count = len(shape)
    return (
        shaped((slots,) + tuple(shape), dtype),
        pl.BlockSpec((None,) + tuple(shape), lambda s, sc: (s,) + (0,) * count),
    )


def full_out(shape, dtype):
    count = len(shape)
    return shaped(shape, dtype), pl.BlockSpec(tuple(shape), lambda s, sc: (0,) * count)


def call(kernel, steps, scalars, inputs, outs, scratch=(), flops=0):
    inputs = [a if isinstance(a, tuple) else (a, whole(a)) for a in inputs]
    arrays, specs = zip(*inputs)
    shapes, out_specs = zip(*outs)
    moved = sum(a.size * a.dtype.itemsize for a in arrays + shapes)
    return pl.pallas_call(
        kernel,
        grid_spec=pltpu.PrefetchScalarGridSpec(
            num_scalar_prefetch=1,
            grid=(steps,),
            in_specs=list(specs),
            out_specs=list(out_specs),
            scratch_shapes=list(scratch),
        ),
        out_shape=list(shapes),
        cost_estimate=pl.CostEstimate(flops=flops, bytes_accessed=moved, transcendentals=0),
    )(scalars, *arrays)


def call_once(kernel, scalars, inputs, outs, scratch=()):
    moved = sum(a.size * a.dtype.itemsize for a in list(inputs) + list(outs))
    space = pl.BlockSpec(memory_space=pltpu.VMEM)
    first = [] if scalars is None else [scalars]
    return pl.pallas_call(
        kernel,
        in_specs=[pl.BlockSpec(memory_space=pltpu.SMEM)] * len(first) + [space] * len(inputs),
        out_specs=[space] * len(outs),
        out_shape=list(outs),
        scratch_shapes=list(scratch),
        cost_estimate=pl.CostEstimate(flops=0, bytes_accessed=moved, transcendentals=0),
    )(*first, *inputs)


def tie(first, second):
    return lax.optimization_barrier((first, second))


def gather_rows(value):
    for bit in frame_bits(GROUP):
        value = jnp.concatenate([value, swap_frames(value, bit)], axis=0)
    value = jnp.concatenate([value, swap_frames(value, 1)], axis=0)
    return [value] + [swap_frames(value, bit) for bit in (2, 4, 6)]


def gathered_places(frame_index):
    count = lax.axis_size("frames")
    far = jnp.arange(count // GROUP) * GROUP
    near = jnp.arange(GROUP)
    return frame_index ^ (near.reshape(4, 2, 1) + far).reshape(-1)


def gather_halves(first, second):
    first = jnp.stack([first, swap_frames(first, 2)])
    second = jnp.stack([second, swap_frames(second, 4)])
    first_far = swap_frames(first, 4)
    second_far = swap_frames(second, 2)
    near = jnp.stack(
        [
            jnp.concatenate([first, first_far], axis=0),
            jnp.concatenate([second, second_far], axis=0),
        ]
    )
    return near, swap_frames(near, 1)


def reduce_first(keep, got):
    half = keep.shape[4] // 2

    def summed(x, y, low):
        rows = slice(0, half) if low else slice(half, 2 * half)
        index = (x, y, slice(None), slice(None), rows)
        return keep[index].astype(f32) + got[index].astype(f32)

    both = slice(None)
    first_got = swap_frames(summed(1, both, True).astype(bf16), 2)
    second_got = swap_frames(summed(both, 1, False).astype(bf16), 4)
    return summed, first_got, second_got


def reduce_second(summed, first_got, second_got):
    def next_first(y):
        return summed(0, y, True) + first_got[y].astype(f32)

    def next_second(x):
        return summed(x, 0, False) + second_got[x].astype(f32)

    first_last = swap_frames(next_first(1).astype(bf16), 4)
    second_last = swap_frames(next_second(1).astype(bf16), 2)
    return next_first(0), next_second(0), first_last, second_last


def reduce_last(first, second, first_last, second_last):
    def quarter(slot):
        low = first[slot] + first_last[slot].astype(f32)
        high = second[slot] + second_last[slot].astype(f32)
        value = jnp.concatenate([low, high], axis=1)
        return value.reshape(-1, value.shape[2])

    quarters = [quarter(s) for s in range(first.shape[0])]
    for bit in frame_bits(GROUP):
        quarters = [q + swap_frames(q.astype(bf16), bit).astype(f32) for q in quarters]
    own = quarters[0]
    for step in range(1, len(quarters)):
        own = own + to_heads(quarters[step].astype(bf16), -step).astype(f32)
    return own.astype(bf16)


def regather(rows):
    half = rows.shape[0] // 2
    first, second = rows[:half], rows[half:]
    first = jnp.stack([first, swap_frames(first, 2)])
    second = jnp.stack([second, swap_frames(second, 4)])
    first = jnp.concatenate([first, swap_frames(first, 4)], axis=0)
    second = jnp.concatenate([second, swap_frames(second, 2)], axis=0)
    second = jnp.stack([second[0], second[2], second[1], second[3]])
    near = jnp.concatenate([first, second], axis=1)
    return near, swap_frames(near, 1)


def on_device(
    frames_in,
    upstream,
    video_of_frame,
    group_ids,
    msg_fc_weight,
    msg_fc_bias,
    msg_gain,
    msg_shift,
    msg_qkv_weight,
    msg_qv_bias,
    courier_result_kernel,
    msg_out_bias,
    ln1_gain,
    ln1_shift,
    qkv_weight,
    qv_bias,
    picture_result_kernel,
    out_bias,
    ln2_gain,
    ln2_shift,
    fc_weight,
    fc_bias,
    proj_weight,
    proj_bias,
):
    block, patches, local = frames_in.shape
    width = msg_qkv_weight.shape[0]
    slots = lax.axis_size("heads")
    own_frames = block // slots
    heads = local // HS
    tokens = -(-(patches + 1) // 16) * 16
    rows = own_frames * tokens
    hidden_local = fc_weight.shape[1]
    share = width // GROUP
    frame_index = lax.axis_index("frames")
    head_index = lax.axis_index("heads")
    place = frame_index % GROUP
    scalars = jnp.stack([head_index, place]).astype(jnp.int32)
    steps = range(1, slots)
    turned = pltpu.VMEM((width, 256), bf16)
    frame_spec = pl.BlockSpec((own_frames, local, patches), lambda s, sc: (sc[0], 0, 0))

    def to_all_heads(value):
        return [value] + [to_heads(value, s) for s in steps]

    def my_rows(array):
        return lax.dynamic_slice_in_dim(array, place * share, share, axis=0)

    x_turned = jnp.transpose(frames_in, (0, 2, 1))
    up_turned = jnp.transpose(upstream, (0, 2, 1))
    msg_qkv = jnp.transpose(msg_qkv_weight, (1, 2, 0))
    sent_rows = SMALL + share + 2 * local // 3
    attn_own, cls_own, send_1, send_2, send_3 = call_once(
        pack_first,
        scalars,
        [x_turned, msg_fc_weight, jnp.transpose(qkv_weight, (1, 2, 0)), picture_result_kernel,
         msg_fc_bias, msg_gain, msg_shift, msg_out_bias, ln1_gain, ln1_shift,
         out_bias, ln2_gain, ln2_shift, proj_bias, qv_bias, fc_bias],
        [shaped((width, width), bf16), shaped((block, local), f32)]
        + [shaped((sent_rows, width), bf16)] * 3,
    )
    received = [send_1] + [to_heads(v, s) for s, v in zip(steps, (send_1, send_2, send_3))]
    nat, fc_bias_slots, qkv_bias_slots, sent, first_half, second_half, stream = call(
        functools.partial(unpack_first, block=block, tokens=tokens),
        1,
        scalars,
        [(x_turned, frame_spec), cls_own] + received,
        [
            full_out((16, width), f32),
            full_out((slots, 1, width), f32),
            full_out((slots, 1, 3 * local), f32),
            full_out((block, 1024), f32),
            full_out((slots - 1, 1, share // 2, width), bf16),
            full_out((slots - 1, 1, share // 2, width), bf16),
            full_out((rows, width), bf16),
        ],
        [turned],
    )
    start_pieces = gather_rows(sent)
    attn_near, attn_far = gather_halves(first_half, second_half)
    mine = jnp.stack([my_rows(fc_weight), my_rows(proj_weight)])
    mine, start_pieces = tie(mine, start_pieces)
    got = [to_heads(mine, s) for s in steps]
    mlp_near, mlp_far = gather_halves(
        jnp.stack([g[:, : share // 2] for g in got]), jnp.stack([g[:, share // 2 :] for g in got])
    )
    attn_weights = list(
        zip((attn_own, attn_near, attn_far), weight_specs(attn_own, attn_near, 0))
    )
    mlp_weights = list(
        zip(
            (fc_weight, mlp_near, mlp_far, proj_weight, mlp_near, mlp_far),
            weight_specs(fc_weight, mlp_near, 0) + weight_specs(proj_weight, mlp_near, 1),
        )
    )

    ids = video_of_frame.reshape(-1, block)[gathered_places(frame_index)].reshape(-1)
    ids_row, ids_col = ids[None, :], ids[:, None]
    total_frames = ids.shape[0]
    start, cls_all, msg_rows, msg_proj, msg_probs, msg_context, msg_part = call_once(
        functools.partial(message_forward, heads=heads, block=block),
        None,
        list(start_pieces) + [ids_col, ids_row, nat, msg_qkv, msg_qv_bias, courier_result_kernel],
        [
            shaped((total_frames, width), f32),
            shaped((total_frames, local), bf16),
            shaped((total_frames, width), bf16),
            shaped((total_frames, 3 * local), bf16),
            shaped((heads, total_frames, total_frames), f32),
            shaped((total_frames, local), bf16),
            shaped((block, width), f32),
        ],
    )
    msg_parts = to_all_heads(msg_part)

    qkv, probs, context, stream_one, normed_one, stream_two = call(
        functools.partial(attention_forward, heads=heads, tokens=tokens, patches=patches),
        slots,
        scalars,
        [stream]
        + msg_parts
        + [(start, first_rows(start, block)), nat, (qkv_bias_slots, per_slot(qkv_bias_slots))]
        + attn_weights,
        [
            slot_out((rows, 3 * local), bf16, slots),
            slot_out((own_frames * heads, tokens, tokens), bf16, slots),
            slot_out((rows, local), bf16, slots),
            full_out((rows, width), f32),
            full_out((rows, width), bf16),
            full_out((rows, width), f32),
        ],
        [pltpu.VMEM((width, width), bf16), pltpu.VMEM((rows, width), f32)],
        2 * rows * width * width * slots,
    )

    frame_out = full_out((own_frames, local, patches), bf16)
    pre, out_0, out_1, out_2, out_3, cls_block = call(
        functools.partial(mlp_forward, block=block, tokens=tokens),
        slots,
        scalars,
        [stream_two, nat, (fc_bias_slots, per_slot(fc_bias_slots))] + mlp_weights,
        [slot_out((rows, hidden_local), f32, slots)]
        + [frame_out] * slots
        + [full_out((block, width), f32)],
        [
            pltpu.VMEM((rows, width), bf16),
            pltpu.VMEM((width, hidden_local), bf16),
            pltpu.VMEM((hidden_local, width), bf16),
            pltpu.VMEM((rows, width), f32),
            turned,
        ],
        4 * rows * width * hidden_local * slots,
    )

    cls_pieces = gather_rows(sum(to_all_heads(cls_block)))
    videos = group_ids.shape[0]
    groups = jnp.pad(group_ids, (0, -videos % 8), constant_values=-1)
    loss_value, cls_grad = call_once(
        functools.partial(contrast, videos=videos, block=block),
        None,
        cls_pieces + [ids_row, ids_col, groups[:, None], groups[None, :]],
        [shaped((1, 1), f32), shaped((block, width), f32)],
    )

    def frames_of(array, step):
        start = jnp.mod(head_index + step, slots) * own_frames
        return lax.dynamic_slice_in_dim(array, start, own_frames, axis=0)

    up_pieces = [(up_turned, frame_spec)] + [to_heads(frames_of(up_turned, s), s) for s in steps]
    out_pieces = [out_0] + [to_heads(o, s) for s, o in zip(steps, (out_1, out_2, out_3))]

    def grad_out(matrices, size):
        shape = (2, 2, slots, matrices, size, width)
        return shaped(shape, bf16), pl.BlockSpec(
            (2, 2, None, matrices, size, width), lambda s, sc: (0, 0, s, 0, 0, 0)
        )

    keep, send, fc_bias_grad, mlp_vec, grad_two = call(
        functools.partial(mlp_backward, tokens=tokens),
        slots,
        scalars,
        up_pieces + [cls_grad, stream_two, (pre, per_slot(pre)), nat] + mlp_weights,
        [
            grad_out(2, share),
            grad_out(2, share),
            slot_out((1, hidden_local), f32, slots),
            full_out((8, width), f32),
            full_out((rows, width), f32),
        ],
        [
            pltpu.VMEM((rows, width), bf16),
            pltpu.VMEM((rows, width), f32),
            pltpu.VMEM((width, hidden_local), bf16),
            pltpu.VMEM((hidden_local, width), bf16),
            pltpu.VMEM((rows, width), f32),
            turned,
        ],
        8 * rows * width * hidden_local * slots,
    )
    mlp_got = swap_frames(send, 1)

    dproj, vec, gi_0, gi_1, gi_2, gi_3, grad_msg_block = call(
        functools.partial(attention_backward, heads=heads, block=block, tokens=tokens),
        slots,
        scalars,
        [grad_two, stream_one, (qkv, per_slot(qkv)), (probs, per_slot(probs)), nat, mlp_vec, fc_bias_grad]
        + attn_weights,
        [slot_out((rows, 3 * local), bf16, slots), full_out((slots, 8, width), f32)]
        + [frame_out] * slots
        + [full_out((block, width), f32)],
        [
            pltpu.VMEM((rows, width), bf16),
            pltpu.VMEM((8, width), f32),
            pltpu.VMEM((width, width), bf16),
            pltpu.VMEM((rows, width), f32),
            turned,
        ],
        6 * rows * width * width * slots,
    )
    dproj, mlp_got = tie(dproj, mlp_got)
    mlp_state = reduce_first(keep, mlp_got)
    attn_keep, attn_send = call(
        attention_weights,
        slots,
        scalars,
        [grad_two, normed_one, (dproj, per_slot(dproj)), (context, per_slot(context)), (vec, per_slot(vec))],
        [grad_out(1, share + 16), grad_out(1, share + 16)],
        [pltpu.VMEM((rows, width), bf16)],
        2 * rows * width * width * slots,
    )
    attn_got = swap_frames(attn_send, 1)
    msg_pieces = gather_rows(sum(to_all_heads(grad_msg_block)))
    vector = shaped((local,), f32)
    (
        grad_message, grad_msg_qkv, grad_msg_out_weight, back_own, back_send, grad_msg_out_bias,
        grad_msg_qv_bias,
    ) = call_once(
        functools.partial(message_back_one, heads=heads),
        scalars,
        msg_pieces + [msg_rows, msg_proj, msg_probs, msg_context, msg_qkv, courier_result_kernel],
        [
            shaped((total_frames, width), f32),
            shaped((3, local, width), f32),
            shaped((local, width), f32),
            shaped((total_frames, width), f32),
            shaped((total_frames, width), bf16),
            vector,
            shaped((2, local), f32),
        ],
    )
    back = [back_own] + [to_heads(back_send, s) for s in steps]
    grad_msg_fc_weight, grad_msg_gain, grad_msg_shift, grad_msg_fc_bias, cls_back = call_once(
        message_back_two,
        scalars,
        back + [grad_message, start, cls_all, nat, msg_fc_weight],
        [shaped((local, width), f32), vector, vector, vector, shaped((local, 16), f32)],
    )
    grad_pieces = [gi_0] + [to_heads(g, s) for s, g in zip(steps, (gi_1, gi_2, gi_3))]

    mlp_state = reduce_second(*mlp_state)
    attn_state = reduce_second(*reduce_first(attn_keep, attn_got))
    near, far = regather(
        jnp.concatenate([reduce_last(*mlp_state), reduce_last(*attn_state)], axis=0)
    )

    def picked(s, sc):
        return ((s ^ sc[1]) // 2, 0, 0)

    part_spec = pl.BlockSpec((None,) + near.shape[1:], picked)
    flat = shaped((width, width), f32)
    flat_spec = pl.BlockSpec((share, width), lambda s, sc: (s, 0))
    grad_fc_weight, grad_proj_weight, grad_qkv, grad_out_weight, vectors = call(
        functools.partial(finish_weights, block=share),
        GROUP,
        scalars,
        [(near, part_spec), (far, part_spec)],
        [
            (flat, flat_spec),
            (flat, flat_spec),
            (
                shaped((3 * local, width), f32),
                pl.BlockSpec((share, width), lambda s, sc: (jnp.minimum(s, 5), 0)),
            ),
            (
                shaped((local, width), f32),
                pl.BlockSpec((share, width), lambda s, sc: (jnp.maximum(s - 6, 0), 0)),
            ),
            full_out((8, width), f32),
        ],
    )
    *features, grad_fc_bias, grad_qv_bias = call_once(
        finish_vectors,
        scalars,
        [vectors],
        [vector] * 6 + [shaped((width,), f32), shaped((2, local), f32)],
    )
    (output,) = call_once(
        finish_output, scalars, out_pieces, [shaped((block, local, patches), bf16)]
    )
    (grad_input,) = call_once(
        finish_grads, scalars, grad_pieces + [cls_back], [shaped((block, local, patches), f32)]
    )
    return (
        jnp.transpose(output, (0, 2, 1)),
        loss_value.reshape(()),
        jnp.transpose(grad_input, (0, 2, 1)),
        grad_msg_fc_weight,
        grad_msg_fc_bias,
        grad_msg_gain,
        grad_msg_shift,
        jnp.transpose(grad_msg_qkv, (2, 0, 1)),
        grad_msg_qv_bias,
        grad_msg_out_weight,
        grad_msg_out_bias,
        features[0],
        features[1],
        jnp.transpose(grad_qkv.reshape(3, local, width), (2, 0, 1)),
        grad_qv_bias,
        grad_out_weight,
        features[2],
        features[3],
        features[4],
        grad_fc_weight,
        grad_fc_bias,
        grad_proj_weight,
        features[5],
    )


def solution(mesh):
    placed = (
        P("frames", None, "heads"),
        P("frames", None, "heads"),
        P(),
        P(),
        P("heads", None),
        P("heads"),
        P("heads"),
        P("heads"),
        P(None, None, "heads"),
        P(None, "heads"),
        P("heads", None),
        P("heads"),
        P("heads"),
        P("heads"),
        P(None, None, "heads"),
        P(None, "heads"),
        P("heads", None),
        P("heads"),
        P("heads"),
        P("heads"),
        P(None, "heads"),
        P("heads"),
        P("heads", None),
        P("heads"),
    )
    return jax.shard_map(
        on_device,
        mesh=mesh,
        in_specs=placed,
        out_specs=(
            P("frames", None, "heads"),
            P(),
            P("frames", None, "heads"),
            P("heads", None),
            P("heads"),
            P("heads"),
            P("heads"),
            P(None, None, "heads"),
            P(None, "heads"),
            P("heads", None),
            P("heads"),
            P("heads"),
            P("heads"),
            P(None, None, "heads"),
            P(None, "heads"),
            P("heads", None),
            P("heads"),
            P("heads"),
            P("heads"),
            P(None, "heads"),
            P("heads"),
            P("heads", None),
            P("heads"),
        ),
        check_vma=False,
    )
```
